256 devices in a mesh: dp: 16 (over y, x), cluster: 16 (over z, core).
Axes of the slice: x: 4, y: 4, z: 8, core: 2. Of those that a mesh axis runs over, the one named last changes fastest.
Arguments:
- points: bfloat16 [524288, 768], P(('dp', 'cluster')), may hold values from -12 to 12
- coarse_id: int32 [524288, 1], P(('dp', 'cluster')), may hold values from 0 to 255; in each aligned block of 2048 rows (0 to 2047, 2048 to 4095, ...) at most 24 rows name the same one
- owner_map: int32 [256], replicated, may hold values from 0 to 255, each once
- centroids: bfloat16 [256, 256, 768], P('cluster', 'dp'), may hold values from -1 to 1
Outputs:
- new_centroids: bfloat16 [256, 256, 768], P('cluster', 'dp')
- point_score: float32 [524288], P(('dp', 'cluster'))
The draws below stay inside these ranges and needn't reach their ends.
Inputs may be any that keep to these rules, and one draw needn't show every extreme that they name: `coarse_id`: in the rows of one device no coarse cluster appears more than 24 times, and some cluster appears exactly 24 times. `owner_map`: a permutation; slot s lies on cluster index s // 16.
All inputs are finite; a program needn't handle non-finite values.
Results may differ from the reference program's by a relative error of at most 0.007.
Values may be sent and summed in bfloat16 or wider, within the bound.
No kernel may reach another device: no remote copies, remote signals or barrier semaphores. Data moves between devices by JAX's collectives and lax.ppermute only.
A program may use at most 128 MiB of HBM per device.

```python
import math
import jax
import jax.numpy as jnp
import numpy as np
from jax import lax

D = 768
F = 256
PTS_DEV = 2048
K = 256
POINTS = 524288
CAPK = 24
N_DP = 16
N_CLUSTER = 16


def draw_centroids(key, part):
    spread = 2.8 / math.sqrt(D)
    values_base = jax.random.normal(jax.random.fold_in(key, 11), (K, F, D), jnp.float32) * spread
    return jnp.clip(values_base, -1.0, 1.0).astype(jnp.bfloat16)


def draw_points(key, part):
    values_base = jax.random.normal(jax.random.fold_in(key, 15), (POINTS, D), jnp.float32)
    return jnp.clip(values_base, -12.0, 12.0).astype(jnp.bfloat16)


def shared_out(key, own, number, rows, count, top, reach, skew):
    sequence = jax.random.permutation(key, count)
    heavy_load, usual = load_shares(count, rows * top, reach, skew, True), load_shares(count, rows * top, reach, skew, False)
    places = jnp.arange(count)

    def named(lengths, offset_by):
        used = int((lengths > 0).sum())
        fixed = max(1, used // 4)
        moved = fixed + (places - fixed + offset_by * (used - fixed)) % max(1, count - fixed)
        return jnp.zeros((count,), jnp.int32).at[sequence[jnp.where(places < fixed, places, moved)]].set(jnp.asarray(lengths, jnp.int32))

    lengths = jnp.where(number % 4 == 0, named(heavy_load, number // 4), named(usual, number - number // 4 - 1))
    mixed = jax.random.permutation(jax.random.fold_in(own, 3), count)
    donor, sink = mixed[0:count // 2 * 2:2], mixed[1:count // 2 * 2:2]
    room = jnp.minimum(lengths[donor] - 1, reach - lengths[sink]) // 2
    room = jnp.where((donor == sequence[0]) | (sink == sequence[0]) | (lengths[sink] == 0), 0, jnp.maximum(room, 0))
    moved = jax.random.randint(jax.random.fold_in(own, 4), (count // 2,), 0, 1 << 20) % (room + 1)
    lengths = lengths.at[donor].add(-moved).at[sink].add(moved)
    labels = jnp.searchsorted(jnp.cumsum(lengths), jnp.arange(rows * top), side="right").astype(jnp.int32)
    table = labels.reshape(top, rows).T
    table = table[jax.random.permutation(jax.random.fold_in(own, 1), rows)]
    offset_by = jax.random.randint(jax.random.fold_in(own, 2), (rows, 1), 0, top)
    return jnp.take_along_axis(table, (jnp.arange(top)[None, :] + offset_by) % top, axis=1)


def load_shares(amount, total, limit, slope, full):
    loads = [(1 << 20) // math.isqrt(rank ** slope) + 1 for rank in range(1, amount + 1)]
    largest = limit if full else min(limit, max(-(-total // amount), total * loads[0] // sum(loads)))
    least = 1 if total - largest >= amount - 1 else 0
    given, surplus = [largest] + [least] * (amount - 1), total - largest - least * (amount - 1)
    while surplus > 0:
        movable = [i for i in range(1, amount) if given[i] < largest] or [i for i in range(1, amount) if given[i] < limit]
        mass, left = sum([loads[i] for i in movable]), surplus
        for i in movable:
            addition = min(limit - given[i], max(1, left * loads[i] // mass), surplus)
            given[i] = given[i] + addition
            surplus = surplus - addition
    return np.array(given)


def setup_inputs(seed: int = 0) -> dict:
    streams_of = jax.random.split(jax.random.key(seed), 5)
    points = draw_points(jax.random.fold_in(streams_of[4], 71), 0)
    coarse_id_keys = jax.random.split(jax.random.fold_in(streams_of[1], 1), POINTS // PTS_DEV)
    coarse_id_turns = jax.random.permutation(jax.random.fold_in(streams_of[1], 3), POINTS // PTS_DEV)
    coarse_id = jax.vmap(lambda own, number: shared_out(jax.random.fold_in(streams_of[1], 2), own, number, PTS_DEV, K, 1, CAPK, 2))(coarse_id_keys, coarse_id_turns).reshape((POINTS, 1))
    owner_map = jax.random.permutation(streams_of[2], K).astype(jnp.int32)
    centroids = draw_centroids(jax.random.fold_in(streams_of[4], 71), 0)
    return dict(points=points, coarse_id=coarse_id, owner_map=owner_map, centroids=centroids)


prior_mass = 4.0


def reference(points, coarse_id, owner_map, centroids):
    count_all = points.shape[0]
    window = CAPK * N_DP * N_CLUSTER
    slot_index = owner_map[coarse_id[:, 0]].astype(jnp.int32)
    sorted_order = jnp.argsort(slot_index, stable=True).astype(jnp.int32)
    sorted_rows = jnp.concatenate([points[sorted_order], jnp.zeros((window, D), jnp.bfloat16)], 0)
    slot_sizes = jnp.sum((slot_index[:, None] == jnp.arange(K, dtype=jnp.int32)[None, :]).astype(jnp.int32), 0).astype(jnp.int32)
    starts = (jnp.cumsum(slot_sizes) - slot_sizes).astype(jnp.int32)

    def per_panel(panel_index):
        slot_start = starts[panel_index]
        slot_size = slot_sizes[panel_index]
        window_rows = lax.dynamic_slice_in_dim(sorted_rows, slot_start, window, 0)
        panel_rows = centroids[panel_index]
        sqnorm = jnp.sum(jnp.square(panel_rows.astype(jnp.float32)), -1)
        logits = jnp.dot(window_rows, panel_rows.T, preferred_element_type=jnp.float32) - 0.5 * sqnorm[None, :]
        row_peak = jnp.max(logits, -1, keepdims=True)
        shifted = jnp.exp(logits - row_peak)
        row_total = jnp.sum(shifted, -1, keepdims=True)
        log_total = row_peak[:, 0] + jnp.log(row_total[:, 0])
        live_rows = (jnp.arange(window, dtype=jnp.int32) < slot_size).astype(jnp.bfloat16)
        weights_bf = (shifted / row_total).astype(jnp.bfloat16) * live_rows[:, None]
        sums = jnp.dot(weights_bf.T, window_rows, preferred_element_type=jnp.float32)
        counts = jnp.sum(weights_bf.astype(jnp.float32), 0)
        updated = ((sums + prior_mass * panel_rows.astype(jnp.float32)) / (counts[:, None] + prior_mass)).astype(jnp.bfloat16)
        return updated, log_total

    updated, score_rows = lax.map(per_panel, jnp.arange(K, dtype=jnp.int32))
    position = starts[:, None] + jnp.arange(window, dtype=jnp.int32)[None, :]
    live_all = jnp.arange(window, dtype=jnp.int32)[None, :] < slot_sizes[:, None]
    target = jnp.where(live_all, position, count_all).astype(jnp.int32)
    sorted_score = jnp.zeros((count_all + 1,), jnp.float32).at[target.reshape(-1)].set(score_rows.reshape(-1))
    point_score = jnp.zeros((count_all,), jnp.float32).at[sorted_order].set(sorted_score[:count_all])
    return updated, point_score
```

```python
import functools
import jax
import jax.numpy as jnp
from jax import lax
from jax.experimental import pallas as pl
from jax.experimental.pallas import tpu as pltpu
from jax.sharding import Mesh, PartitionSpec as P

PRIOR = 4.0
CAP = 24
ROWS = 128
PLANE = ("y", "x", "core")
BF = jnp.bfloat16
F32 = jnp.float32


def iota(shape, dim):
    return lax.broadcasted_iota(jnp.int32, shape, dim)


def dot(a, b, dims=((1,), (0,))):
    return lax.dot_general(a, b, (dims, ((), ())), preferred_element_type=F32)


def onehot(mask):
    return jnp.where(mask, 1.0, 0.0).astype(BF)


def index_kernel(zn, dpn, cores, bound, coarse_ref, owner_ref, place_ref, count_ref, hot_ref):
    slots = owner_ref.shape[1]
    rows = coarse_ref.shape[1]
    owner = owner_ref[...]
    column, cluster = owner % dpn, owner // dpn
    lane_of = (column * cores + cluster % cores) * zn + cluster // cores
    move = onehot(iota((slots, slots), 0) == lane_of)
    blk = 256
    earlier = onehot(iota((blk, blk), 0) < iota((blk, blk), 1))
    carry = jnp.zeros((slots, 1), F32)
    ranks = []
    for b in range(rows // blk):
        named = onehot(iota((slots, blk), 0) == coarse_ref[:, b * blk : (b + 1) * blk])
        hot = dot(move, named)
        hot_bf = hot.astype(BF)
        hot_ref[:, b * blk : (b + 1) * blk] = hot_bf
        before = dot(hot_bf, earlier) + carry
        ranks.append(jnp.sum(hot * before, axis=0, keepdims=True))
        carry = carry + jnp.sum(hot, axis=1, keepdims=True)
    rank = jnp.concatenate(ranks, axis=1)
    hot_all = hot_ref[...]
    counts = dot(jnp.ones((8, rows), BF), hot_all, ((1,), (1,)))
    la, lb = iota((slots, slots), 0), iota((slots, slots), 1)
    group = onehot((la // zn == lb // zn) & (la < lb))
    offset = dot(counts.astype(BF), group)
    which = iota((8, slots), 0)
    query = jnp.where(which == 0, offset, iota((8, slots), 1).astype(F32)).astype(BF)
    found = dot(query, hot_all)
    lane = found[1:2].astype(jnp.int32)
    rank = rank.astype(jnp.int32)
    pos = (lane // zn) * bound + found[0:1].astype(jnp.int32) + rank
    row = iota((8, rows), 0)
    place_ref[...] = jnp.where(row == 0, pos, jnp.where(row == 1, lane, rank))
    count_ref[...] = counts.astype(jnp.int32)


def index(coarse, owner, zn, dpn, cores, bound):
    rows, slots = coarse.shape[1], owner.shape[1]
    return pl.pallas_call(
        functools.partial(index_kernel, zn, dpn, cores, bound),
        out_shape=(
            jax.ShapeDtypeStruct((8, rows), jnp.int32),
            jax.ShapeDtypeStruct((8, slots), jnp.int32),
        ),
        scratch_shapes=[pltpu.VMEM((slots, rows), BF)],
        cost_estimate=pl.CostEstimate(flops=10**9, bytes_accessed=10**5, transcendentals=0),
        name="place",
    )(coarse, owner)


def pack_kernel(per, first, bound, place_ref, points_ref, out_ref):
    g = pl.program_id(0)
    tall = out_ref.shape[0]
    i = iota((tall, 1), 0)
    want = (g * (tall // per) + i // per) * bound + first + i % per
    pick = onehot(place_ref[0:1, :] == want)
    out_ref[...] = dot(pick, points_ref[...]).astype(BF)


def pack(place, points, peers, per, first, bound):
    rows, width = points.shape
    tall = 256
    return pl.pallas_call(
        functools.partial(pack_kernel, per, first, bound),
        grid=(peers * per // tall,),
        in_specs=[
            pl.BlockSpec((8, rows), lambda g: (0, 0)),
            pl.BlockSpec((rows, width), lambda g: (0, 0)),
        ],
        out_specs=pl.BlockSpec((tall, width), lambda g: (g, 0)),
        out_shape=jax.ShapeDtypeStruct((peers * per, width), BF),
        cost_estimate=pl.CostEstimate(
            flops=2 * peers * per * rows * width, bytes_accessed=10**7, transcendentals=0
        ),
        name="pack",
    )(place, points)


def assign_kernel(
    pairs, zn, flag_ref, dest_ref, more_dest_ref, live_ref, in_ref, more_ref, panel_ref,
    sums_ref, mass_ref, score_ref, held, more_vmem,
):
    g = pl.program_id(0)
    pad = 2 * CAP

    @pl.when(g < pairs)
    def _():
        tall = zn * pad
        pick = onehot(iota((tall, in_ref.shape[0]), 0) == dest_ref[pl.ds(g, 1), :])
        laid = dot(pick, in_ref[...]).astype(BF)
        start = pl.multiple_of(g * pad, 16)
        for j in range(zn):
            held[j, pl.ds(start, pad), :] = laid[j * pad : (j + 1) * pad]

        @pl.when(flag_ref[0] != 0)
        def _():
            deep = more_vmem.shape[0]
            pltpu.sync_copy(more_ref.at[pl.ds(pl.multiple_of(g * deep, deep), deep), :], more_vmem)
            pick = onehot(iota((tall, deep), 0) == more_dest_ref[pl.ds(g, 1), :])
            more = dot(pick, more_vmem[...])
            for j in range(zn):
                old = held[j, pl.ds(start, pad), :].astype(F32)
                held[j, pl.ds(start, pad), :] = (old + more[j * pad : (j + 1) * pad]).astype(BF)

    @pl.when(g >= pairs)
    def _():
        j = g - pairs
        x = held[j]
        panel = panel_ref[0]
        wide = panel.astype(F32)
        sqnorm = jnp.sum(wide * wide, axis=1, keepdims=True)
        logits = dot(panel, x, ((1,), (1,))) - 0.5 * sqnorm
        peak = jnp.max(logits, axis=0, keepdims=True)
        shifted = jnp.exp(logits - peak)
        total = jnp.sum(shifted, axis=0, keepdims=True)
        score_ref[pl.ds(j, 1), :] = peak + jnp.log(total)
        live = live_ref[pl.ds(j, 1), :]
        weights = jnp.where(live > 0, shifted * (1.0 / total), 0.0).astype(BF)
        sums_ref[0] = dot(weights, x).astype(BF)
        mass = dot(jnp.ones((8, x.shape[0]), BF), weights, ((1,), (1,)))
        mass_ref[pl.ds(j, 1), :] = mass[0:1]


def assign(flag, dest, more_dest, live, rows, more, panels):
    zn, fine, width = panels.shape
    pairs, deep = dest.shape
    more_deep = more_dest.shape[1]
    spread = pairs * 2 * CAP
    last = pairs - 1
    whole = lambda g, f: (0, 0)
    return pl.pallas_call(
        functools.partial(assign_kernel, pairs, zn),
        grid_spec=pltpu.PrefetchScalarGridSpec(
            num_scalar_prefetch=1,
            grid=(pairs + zn,),
            in_specs=[
                pl.BlockSpec((pairs, deep), whole),
                pl.BlockSpec((pairs, more_deep), whole),
                pl.BlockSpec((zn, spread), whole),
                pl.BlockSpec((deep, width), lambda g, f: (jnp.minimum(g, last), 0)),
                pl.BlockSpec(memory_space=pl.ANY),
                pl.BlockSpec((1, fine, width), lambda g, f: (jnp.maximum(g - pairs, 0), 0, 0)),
            ],
            out_specs=[
                pl.BlockSpec((1, fine, width), lambda g, f: (jnp.maximum(g - pairs, 0), 0, 0)),
                pl.BlockSpec((zn, fine), whole),
                pl.BlockSpec((zn, spread), whole),
            ],
            scratch_shapes=[
                pltpu.VMEM((zn, spread, width), BF),
                pltpu.VMEM((more_deep, width), BF),
            ],
        ),
        out_shape=(
            jax.ShapeDtypeStruct((zn, fine, width), BF),
            jax.ShapeDtypeStruct((zn, fine), F32),
            jax.ShapeDtypeStruct((zn, spread), F32),
        ),
        compiler_params=pltpu.CompilerParams(vmem_limit_bytes=48 * 2**20),
        cost_estimate=pl.CostEstimate(
            flops=8 * 10**9, bytes_accessed=2 * 10**7, transcendentals=2 * 10**6
        ),
        name="assign",
    )(flag, dest, more_dest, live, rows, more, panels)


def lookup_kernel(place_ref, table_ref, out_ref):
    slots, rows = table_ref.shape[1], place_ref.shape[1]
    table = table_ref[...]
    hi = table.astype(BF)
    rest = table - hi.astype(F32)
    mid = rest.astype(BF)
    low = (rest - mid.astype(F32)).astype(BF)
    hot = onehot(iota((slots, rows), 0) == place_ref[1:2, :])
    value = dot(hi, hot) + dot(mid, hot) + dot(low, hot)
    mine = iota(value.shape, 0) == place_ref[2:3, :]
    out_ref[...] = jnp.sum(jnp.where(mine, value, 0.0), axis=0, keepdims=True)


def lookup(place, table):
    return pl.pallas_call(
        lookup_kernel,
        out_shape=jax.ShapeDtypeStruct((1, place.shape[1]), F32),
        cost_estimate=pl.CostEstimate(flops=10**8, bytes_accessed=10**5, transcendentals=0),
        name="lookup",
    )(place, table)


def exchange(x, axes):
    return lax.all_to_all(x, axes, split_axis=0, concat_axis=0, tiled=True)


def local(points, coarse_id, owner_map, centroids):
    zn, cores = lax.axis_size("z"), lax.axis_size("core")
    dpn = lax.axis_size("y") * lax.axis_size("x")
    peers = dpn * cores
    bound = zn * CAP
    rows, width = points.shape
    per, rest = ROWS, bound - ROWS

    panel = exchange(centroids, ("y", "x")).reshape(-1, width)
    place, counts = index(coarse_id.reshape(1, rows), owner_map.reshape(1, -1), zn, dpn, cores, bound)
    packed = pack(place, points, peers, per, 0, bound).reshape(peers, per, width)
    arrived = exchange(packed, PLANE)
    panels = lax.all_gather(panel, "z", axis=0)

    mine = counts[0].reshape(peers, zn)
    most = jnp.max(jnp.sum(mine, axis=1))
    most = jnp.max(exchange(jnp.broadcast_to(most, (zn, 128)), "z"))
    sent = jnp.concatenate([mine, jnp.broadcast_to(most, (peers, zn))], axis=1)
    got = exchange(sent, PLANE)
    over = jnp.max(got[:, zn]) > per
    got = got[:, :zn]
    ends = jnp.cumsum(got, axis=1)
    at = jnp.arange(bound, dtype=jnp.int32)[None, :, None]
    slot_at = jnp.sum((at >= ends[:, None, :]).astype(jnp.int32), axis=2)
    begin = jnp.sum(jnp.where(at >= ends[:, None, :], got[:, None, :], 0), axis=2)
    side = (jnp.arange(peers, dtype=jnp.int32) % 2)[:, None]
    dest = slot_at * (2 * CAP) + side * CAP + at[:, :, 0] - begin
    dest = jnp.where(slot_at < zn, dest, -1)
    live = jnp.arange(CAP, dtype=jnp.int32)[None, None, :] < got.T[:, :, None]
    live = live.astype(F32).reshape(zn, peers * CAP)

    more = lax.cond(
        over,
        lambda: exchange(
            pack(place, points, peers, rest, per, bound).reshape(peers, rest, width), PLANE
        ).reshape(peers * rest, width),
        lambda: jnp.zeros((peers * rest, width), BF),
    )
    sums, mass, score = assign(
        over.astype(jnp.int32).reshape(1),
        dest[:, :per].reshape(peers // 2, 2 * per),
        dest[:, per:].reshape(peers // 2, 2 * rest),
        live,
        arrived.reshape(peers * per, width),
        more,
        panels,
    )
    sums = lax.psum_scatter(sums, "z", scatter_dimension=0, tiled=True)[0]
    score = score.reshape(zn, peers, CAP).transpose(1, 0, 2).reshape(peers, zn * CAP)
    score = exchange(score, PLANE).reshape(peers * zn, CAP).T
    point_score = lookup(place, score).reshape(rows)
    mass = jnp.sum(exchange(mass, "z"), axis=0)
    updated = (sums.astype(F32) + PRIOR * panel.astype(F32)) / (mass[:, None] + PRIOR)
    updated = updated.astype(BF).reshape(dpn, -1, width)
    return exchange(updated, ("y", "x")), point_score


def solution(mesh):
    devices = mesh.devices
    chips = Mesh(devices.reshape(4, 4, 8, 2), ("y", "x", "z", "core"))
    every = ("y", "x", "z", "core")
    grid = P(("z", "core"), ("y", "x"), None)
    return jax.shard_map(
        local,
        mesh=chips,
        in_specs=(P(every, None), P(every, None), P(), grid),
        out_specs=(grid, P(every)),
        check_vma=False,
    )
```

```python
import functools
import jax
import jax.numpy as jnp
from jax import lax
from jax.experimental import pallas as pl
from jax.experimental.pallas import tpu as pltpu
from jax.sharding import Mesh, PartitionSpec as P

PRIOR = 4.0
CAP = 24
ROWS = 128
SOME, REST = 16, 72
PLANE = ("y", "x", "core")
BF = jnp.bfloat16
F32 = jnp.float32


def iota(shape, dim):
    return lax.broadcasted_iota(jnp.int32, shape, dim)


def dot(a, b, dims=((1,), (0,))):
    return lax.dot_general(a, b, (dims, ((), ())), preferred_element_type=F32)


def onehot(mask):
    return jnp.where(mask, 1.0, 0.0).astype(BF)


def index_kernel(zn, dpn, cores, bound, coarse_ref, owner_ref, place_ref, note_ref, hot_ref):
    slots = owner_ref.shape[1]
    rows = coarse_ref.shape[1]
    peers, width = note_ref.shape
    owner = owner_ref[...]
    column, cluster = owner % dpn, owner // dpn
    lane_of = (column * cores + cluster % cores) * zn + cluster // cores
    move = onehot(iota((slots, slots), 0) == lane_of)
    blk = 256
    earlier = onehot(iota((blk, blk), 0) < iota((blk, blk), 1))
    carry = jnp.zeros((slots, 1), F32)
    ranks = []
    for b in range(rows // blk):
        named = onehot(iota((slots, blk), 0) == coarse_ref[:, b * blk : (b + 1) * blk])
        hot = dot(move, named)
        hot_bf = hot.astype(BF)
        hot_ref[:, b * blk : (b + 1) * blk] = hot_bf
        before = dot(hot_bf, earlier) + carry
        ranks.append(jnp.sum(hot * before, axis=0, keepdims=True))
        carry = carry + jnp.sum(hot, axis=1, keepdims=True)
    rank = jnp.concatenate(ranks, axis=1)
    hot_all = hot_ref[...]
    counts = dot(jnp.ones((8, rows), BF), hot_all, ((1,), (1,)))
    la, lb = iota((slots, slots), 0), iota((slots, slots), 1)
    group = onehot((la // zn == lb // zn) & (la < lb))
    offset = dot(counts.astype(BF), group)
    which = iota((8, slots), 0)
    query = jnp.where(which == 0, offset, iota((8, slots), 1).astype(F32)).astype(BF)
    found = dot(query, hot_all)
    lane = found[1:2].astype(jnp.int32)
    rank = rank.astype(jnp.int32)
    pos = (lane // zn) * bound + found[0:1].astype(jnp.int32) + rank
    row = iota((8, rows), 0)
    place_ref[...] = jnp.where(row == 0, pos, jnp.where(row == 1, lane, rank))
    mine = iota((peers, slots), 1) // zn == iota((peers, slots), 0)
    spread = jnp.where(mine, counts[0:1], 0.0)
    most = jnp.max(jnp.sum(spread, axis=1, keepdims=True), axis=0, keepdims=True)
    spot = onehot(iota((slots, width), 0) % zn == iota((slots, width), 1))
    note = dot(spread.astype(BF), spot)
    note_ref[...] = jnp.where(iota((peers, width), 1) == zn, most, note).astype(BF)


def index(coarse, owner, zn, dpn, cores, bound, width):
    rows, slots = coarse.shape[1], owner.shape[1]
    return pl.pallas_call(
        functools.partial(index_kernel, zn, dpn, cores, bound),
        out_shape=(
            jax.ShapeDtypeStruct((8, rows), jnp.int32),
            jax.ShapeDtypeStruct((dpn * cores, width), BF),
        ),
        scratch_shapes=[pltpu.VMEM((slots, rows), BF)],
        cost_estimate=pl.CostEstimate(flops=10**9, bytes_accessed=10**5, transcendentals=0),
        name="place",
    )(coarse, owner)


def pack_kernel(per, first, bound, noted, place_ref, points_ref, note_ref, out_ref):
    g = pl.program_id(0)
    tall = out_ref.shape[0]
    i = iota((tall, 1), 0)
    peer, at = g * (tall // per) + i // per, i % per
    want = peer * bound + first + at
    if noted:
        want = jnp.where(at == per - 1, -1, want)
    pick = onehot(place_ref[0:1, :] == want)
    packed = dot(pick, points_ref[...])
    if noted:
        peers = note_ref.shape[0]
        which = jnp.where(at == per - 1, peer, -1)
        packed = packed + dot(onehot(iota((tall, peers), 1) == which), note_ref[...])
    out_ref[...] = packed.astype(BF)


def pack(place, points, note, per, first, bound, tall, noted):
    rows, width = points.shape
    peers = note.shape[0]
    return pl.pallas_call(
        functools.partial(pack_kernel, per, first, bound, noted),
        grid=(peers * per // tall,),
        in_specs=[
            pl.BlockSpec((8, rows), lambda g: (0, 0)),
            pl.BlockSpec((rows, width), lambda g: (0, 0)),
            pl.BlockSpec((peers, width), lambda g: (0, 0)),
        ],
        out_specs=pl.BlockSpec((tall, width), lambda g: (g, 0)),
        out_shape=jax.ShapeDtypeStruct((peers * per, width), BF),
        cost_estimate=pl.CostEstimate(
            flops=2 * peers * per * rows * width, bytes_accessed=10**7, transcendentals=0
        ),
        name="pack",
    )(place, points, note)


def places(zn, notes, per, first, count):
    lane, sub = iota((zn, 128), 1), iota((zn, 128), 0)
    sides = []
    for note in notes:
        note = jnp.broadcast_to(note, (zn, 128))
        ends = jnp.sum(jnp.where(lane <= sub, note, 0.0), axis=1, keepdims=True)
        size = jnp.sum(jnp.where(lane == sub, note, 0.0), axis=1, keepdims=True)
        sides.append((ends, size))
    c = iota((zn, 2 * per), 1)
    second = c >= per
    at = c - jnp.where(second, per, 0)
    pos = (at + first).astype(F32)
    passed = pos >= jnp.where(second, sides[1][0], sides[0][0])
    size = jnp.where(second, sides[1][1], sides[0][1])
    slot = jnp.sum(jnp.where(passed, 1.0, 0.0), axis=0, keepdims=True)
    begin = jnp.sum(jnp.where(passed, size, 0.0), axis=0, keepdims=True)
    side = jnp.where(second[0:1], 1.0 * CAP, 0.0)
    dest = slot * (2 * CAP) + side + pos[0:1] - begin
    return jnp.where(at[0:1] < count, dest, -1.0).astype(jnp.int32)


def assign_kernel(
    pairs, zn, flag_ref, in_ref, more_ref, panel_ref, sums_ref, mass_ref, score_ref, held, more_vmem
):
    g = pl.program_id(0)
    pad = 2 * CAP
    tall = zn * pad
    width = in_ref.shape[1]
    per, rest = in_ref.shape[0] // 2, more_vmem.shape[0] // 2
    top = zn // 2

    @pl.when(g < pairs)
    def _():
        notes = [in_ref[k * per - 1 : k * per, 0:128].astype(F32) for k in (1, 2)]
        start = pl.multiple_of(g * pad, 16)

        def lay(block, dest, add):
            pick = jnp.where(iota((tall, block.shape[0]), 0) == dest, 1.0, 0.0)
            there = jnp.broadcast_to(jnp.sum(pick, axis=1, keepdims=True), (tall, 128))
            laid = dot(pick.astype(BF), block)
            for j in range(zn):
                part = slice(j * pad, (j + 1) * pad)
                for value, lanes in ((laid[part], slice(0, width)), (there[part], slice(width, width + 128))):
                    if add:
                        value = value + held[j, pl.ds(start, pad), lanes].astype(F32)
                    held[j, pl.ds(start, pad), lanes] = value.astype(BF)

        lay(in_ref[...], places(zn, notes, per, 0, per - 1), False)

        @pl.when(flag_ref[0] != 0)
        def _():
            deep = 2 * rest
            pltpu.sync_copy(more_ref.at[pl.ds(pl.multiple_of(g * deep, 16), deep), :], more_vmem)
            lay(more_vmem[...], places(zn, notes, rest, per - 1, rest), True)

    @pl.when(g >= pairs)
    def _():
        j = g - pairs
        x = held[j]
        panel = panel_ref[0]
        wide = panel.astype(F32)
        sqnorm = jnp.sum(wide * wide, axis=1, keepdims=True)
        logits = dot(panel, x[:, :width], ((1,), (1,))) - 0.5 * sqnorm
        peak = jnp.max(logits, axis=0, keepdims=True)
        shifted = jnp.exp(logits - peak)
        total = jnp.sum(shifted, axis=0, keepdims=True)
        score_ref[pl.ds(j, 1), :] = peak + jnp.log(total)
        weights = (shifted * (1.0 / total)).astype(BF)
        sums = dot(weights, x)
        sums_ref[0] = sums[:, :width].astype(BF)
        mass_ref[pl.ds(j, 1), :] = jnp.transpose(sums[:, width:])[0:1]


def assign(flag, rows, more, panels, pairs):
    zn, fine, width = panels.shape
    deep, more_deep = rows.shape[0] // pairs, more.shape[0] // pairs
    spread = pairs * 2 * CAP
    last = pairs - 1
    whole = lambda g, f: (0, 0)
    return pl.pallas_call(
        functools.partial(assign_kernel, pairs, zn),
        grid_spec=pltpu.PrefetchScalarGridSpec(
            num_scalar_prefetch=1,
            grid=(pairs + zn,),
            in_specs=[
                pl.BlockSpec((deep, width), lambda g, f: (jnp.minimum(g, last), 0)),
                pl.BlockSpec(memory_space=pl.ANY),
                pl.BlockSpec((1, fine, width), lambda g, f: (jnp.maximum(g - pairs, 0), 0, 0)),
            ],
            out_specs=[
                pl.BlockSpec((1, fine, width), lambda g, f: (jnp.maximum(g - pairs, 0), 0, 0)),
                pl.BlockSpec((zn, fine), whole),
                pl.BlockSpec((zn, spread), whole),
            ],
            scratch_shapes=[
                pltpu.VMEM((zn, spread, width + 128), BF),
                pltpu.VMEM((more_deep, width), BF),
            ],
        ),
        out_shape=(
            jax.ShapeDtypeStruct((zn, fine, width), BF),
            jax.ShapeDtypeStruct((zn, fine), F32),
            jax.ShapeDtypeStruct((zn, spread), F32),
        ),
        cost_estimate=pl.CostEstimate(
            flops=8 * 10**9, bytes_accessed=2 * 10**7, transcendentals=2 * 10**6
        ),
        name="assign",
    )(flag, rows, more, panels)


def lookup_kernel(place_ref, table_ref, out_ref):
    slots, rows = table_ref.shape[1], place_ref.shape[1]
    table = table_ref[...]
    hi = table.astype(BF)
    rest = table - hi.astype(F32)
    mid = rest.astype(BF)
    low = (rest - mid.astype(F32)).astype(BF)
    hot = onehot(iota((slots, rows), 0) == place_ref[1:2, :])
    value = dot(hi, hot) + dot(mid, hot) + dot(low, hot)
    mine = iota(value.shape, 0) == place_ref[2:3, :]
    out_ref[...] = jnp.sum(jnp.where(mine, value, 0.0), axis=0, keepdims=True)


def lookup(place, table):
    return pl.pallas_call(
        lookup_kernel,
        out_shape=jax.ShapeDtypeStruct((1, place.shape[1]), F32),
        cost_estimate=pl.CostEstimate(flops=10**8, bytes_accessed=10**5, transcendentals=0),
        name="lookup",
    )(place, table)


def exchange(x, axes):
    return lax.all_to_all(x, axes, split_axis=0, concat_axis=0, tiled=True)


def local(points, coarse_id, owner_map, centroids):
    zn, cores = lax.axis_size("z"), lax.axis_size("core")
    dpn = lax.axis_size("y") * lax.axis_size("x")
    peers = dpn * cores
    bound = zn * CAP
    rows, width = points.shape

    panel = exchange(centroids, ("y", "x")).reshape(-1, width)
    place, note = index(
        coarse_id.reshape(1, rows), owner_map.reshape(1, -1), zn, dpn, cores, bound, width
    )
    packed = pack(place, points, note, ROWS, 0, bound, 1024, True)
    arrived = exchange(packed.reshape(peers, ROWS, width), PLANE)
    panels = lax.all_gather(panel, "z", axis=0)

    most = jnp.max(arrived[:, ROWS - 1, zn].astype(F32))

    def second(per):
        block = pack(place, points, note, per, ROWS - 1, bound, 16 * per, False)
        block = exchange(block.reshape(peers, per, width), PLANE)
        return jnp.pad(block, ((0, 0), (0, REST - per), (0, 0))).reshape(peers * REST, width)

    level = (most > ROWS - 1).astype(jnp.int32) + (most > ROWS - 1 + SOME).astype(jnp.int32)
    more = lax.switch(
        level,
        (lambda: jnp.zeros((peers * REST, width), BF), lambda: second(SOME), lambda: second(REST)),
    )
    sums, mass, score = assign(
        level.reshape(1), arrived.reshape(peers * ROWS, width), more, panels, peers // 2
    )
    sums = lax.psum_scatter(sums, "z", scatter_dimension=0, tiled=True)[0]
    score = score.reshape(zn, peers, CAP).transpose(1, 0, 2).reshape(peers, zn * CAP)
    score = exchange(score, PLANE).reshape(peers * zn, CAP).T
    point_score = lookup(place, score).reshape(rows)
    mass = jnp.sum(exchange(mass, "z"), axis=0)
    updated = (sums.astype(F32) + PRIOR * panel.astype(F32)) / (mass[:, None] + PRIOR)
    updated = updated.astype(BF).reshape(dpn, -1, width)
    return exchange(updated, ("y", "x")), point_score


def solution(mesh):
    devices = mesh.devices
    chips = Mesh(devices.reshape(4, 4, 8, 2), ("y", "x", "z", "core"))
    every = ("y", "x", "z", "core")
    grid = P(("z", "core"), ("y", "x"), None)
    return jax.shard_map(
        local,
        mesh=chips,
        in_specs=(P(every, None), P(every, None), P(), grid),
        out_specs=(grid, P(every)),
        check_vma=False,
    )
```

```python
import functools
import jax
import jax.numpy as jnp
from jax import lax
from jax.experimental import pallas as pl
from jax.experimental.pallas import tpu as pltpu
from jax.sharding import Mesh, PartitionSpec as P

PRIOR = 4.0
CAP = 24
ROWS = 128
SOME, REST = 16, 72
PLANE = ("y", "x", "core")
BF = jnp.bfloat16
F32 = jnp.float32


def iota(shape, dim):
    return lax.broadcasted_iota(jnp.int32, shape, dim)


def dot(a, b, dims=((1,), (0,))):
    return lax.dot_general(a, b, (dims, ((), ())), preferred_element_type=F32)


def onehot(mask):
    return jnp.where(mask, 1.0, 0.0).astype(BF)


def index_kernel(zn, dpn, cores, bound, coarse_ref, owner_ref, place_ref, note_ref, hot_ref):
    slots = owner_ref.shape[1]
    rows = coarse_ref.shape[1]
    peers, width = note_ref.shape
    owner = owner_ref[...]
    column, cluster = owner % dpn, owner // dpn
    lane_of = (column * cores + cluster % cores) * zn + cluster // cores
    move = onehot(iota((slots, slots), 0) == lane_of)
    blk = 256
    earlier = onehot(iota((blk, blk), 0) < iota((blk, blk), 1))
    carry = jnp.zeros((slots, 1), F32)
    ranks = []
    for b in range(rows // blk):
        named = onehot(iota((slots, blk), 0) == coarse_ref[:, b * blk : (b + 1) * blk])
        hot = dot(move, named)
        hot_bf = hot.astype(BF)
        hot_ref[:, b * blk : (b + 1) * blk] = hot_bf
        before = dot(hot_bf, earlier) + carry
        ranks.append(jnp.sum(hot * before, axis=0, keepdims=True))
        carry = carry + jnp.sum(hot, axis=1, keepdims=True)
    rank = jnp.concatenate(ranks, axis=1)
    hot_all = hot_ref[...]
    counts = dot(jnp.ones((8, rows), BF), hot_all, ((1,), (1,)))
    la, lb = iota((slots, slots), 0), iota((slots, slots), 1)
    group = onehot((la // zn == lb // zn) & (la < lb))
    offset = dot(counts.astype(BF), group)
    which = iota((8, slots), 0)
    query = jnp.where(which == 0, offset, iota((8, slots), 1).astype(F32)).astype(BF)
    found = dot(query, hot_all)
    lane = found[1:2].astype(jnp.int32)
    rank = rank.astype(jnp.int32)
    pos = (lane // zn) * bound + found[0:1].astype(jnp.int32) + rank
    row = iota((8, rows), 0)
    place_ref[...] = jnp.where(row == 0, pos, jnp.where(row == 1, lane, rank))
    mine = iota((peers, slots), 1) // zn == iota((peers, slots), 0)
    spread = jnp.where(mine, counts[0:1], 0.0)
    most = jnp.max(jnp.sum(spread, axis=1, keepdims=True), axis=0, keepdims=True)
    spot = onehot(iota((slots, width), 0) % zn == iota((slots, width), 1))
    note = dot(spread.astype(BF), spot)
    note_ref[...] = jnp.where(iota((peers, width), 1) == zn, most, note)


def index(coarse, owner, zn, dpn, cores, bound):
    rows, slots = coarse.shape[1], owner.shape[1]
    return pl.pallas_call(
        functools.partial(index_kernel, zn, dpn, cores, bound),
        out_shape=(
            jax.ShapeDtypeStruct((8, rows), jnp.int32),
            jax.ShapeDtypeStruct((dpn * cores, 128), F32),
        ),
        scratch_shapes=[pltpu.VMEM((slots, rows), BF)],
        cost_estimate=pl.CostEstimate(flops=10**9, bytes_accessed=10**5, transcendentals=0),
        name="place",
    )(coarse, owner)


def pack_kernel(per, first, bound, noted, place_ref, points_ref, note_ref, out_ref):
    g = pl.program_id(0)
    tall, width = out_ref.shape
    i = iota((tall, 1), 0)
    peer, at = g * (tall // per) + i // per, i % per
    want = peer * bound + first + at
    pick = onehot(place_ref[0:1, :] == want)
    packed = dot(pick, points_ref[...])
    out_ref[...] = packed.astype(BF)
    if noted:
        for k in range(tall // per):
            tile = slice((k + 1) * per - 16, (k + 1) * per)
            note = jnp.broadcast_to(note_ref[k : k + 1], (16, 128))
            end = iota((16, 128), 0) == 15
            out_ref[tile, :128] = jnp.where(end, note, packed[tile, :128]).astype(BF)


def pack(place, points, note, per, first, bound, tall, noted):
    rows, width = points.shape
    peers = note.shape[0]
    return pl.pallas_call(
        functools.partial(pack_kernel, per, first, bound, noted),
        grid=(peers * per // tall,),
        in_specs=[
            pl.BlockSpec((8, rows), lambda g: (0, 0)),
            pl.BlockSpec((rows, width), lambda g: (0, 0)),
            pl.BlockSpec((tall // per, 128), lambda g: (g, 0)),
        ],
        out_specs=pl.BlockSpec((tall, width), lambda g: (g, 0)),
        out_shape=jax.ShapeDtypeStruct((peers * per, width), BF),
        cost_estimate=pl.CostEstimate(
            flops=2 * peers * per * rows * width, bytes_accessed=10**7, transcendentals=0
        ),
        name="pack",
    )(place, points, note)


def places(zn, notes, per, first, count):
    lane, sub = iota((zn, 128), 1), iota((zn, 128), 0)
    sides = []
    for note in notes:
        note = jnp.broadcast_to(note, (zn, 128))
        ends = jnp.sum(jnp.where(lane <= sub, note, 0.0), axis=1, keepdims=True)
        size = jnp.sum(jnp.where(lane == sub, note, 0.0), axis=1, keepdims=True)
        sides.append((ends, size))
    c = iota((zn, 2 * per), 1)
    second = c >= per
    at = c - jnp.where(second, per, 0)
    pos = (at + first).astype(F32)
    passed = pos >= jnp.where(second, sides[1][0], sides[0][0])
    size = jnp.where(second, sides[1][1], sides[0][1])
    slot = jnp.sum(jnp.where(passed, 1.0, 0.0), axis=0, keepdims=True)
    begin = jnp.sum(jnp.where(passed, size, 0.0), axis=0, keepdims=True)
    side = jnp.where(second[0:1], 1.0 * CAP, 0.0)
    dest = slot * (2 * CAP) + side + pos[0:1] - begin
    return jnp.where(at[0:1] < count, dest, -1.0).astype(jnp.int32)


def assign_kernel(
    steps, zn, few, slots, flag_ref, in_ref, more_ref, panel_ref, sums_ref, mass_ref, score_ref,
    held, more_vmem,
):
    g = pl.program_id(0)
    pad = 2 * CAP
    tall = zn * pad
    width = in_ref.shape[1]
    deep, more_deep = in_ref.shape[0] // few, more_vmem.shape[0]
    per, rest = deep // 2, more_deep // 2

    def lay(block, dest, start, add):
        pick = jnp.where(iota((tall, block.shape[0]), 0) == dest, 1.0, 0.0)
        there = jnp.broadcast_to(jnp.sum(pick, axis=1, keepdims=True), (tall, 128))
        laid = dot(pick.astype(BF), block)
        for j in range(zn):
            part = slice(j * pad, (j + 1) * pad)
            for value, lanes in ((laid[part], slice(0, width)), (there[part], slice(width, width + 128))):
                if add:
                    value = value + held[j, pl.ds(start, pad), lanes].astype(F32)
                held[j, pl.ds(start, pad), lanes] = value.astype(BF)

    @pl.when(g < steps)
    def _():
        for k in range(few):
            last = [k * deep + per - 1, (k + 1) * deep - 1]
            notes = [in_ref[r : r + 1, 0:128].astype(F32) for r in last]
            start = pl.multiple_of((g * few + k) * pad, 16)
            block = in_ref[k * deep : (k + 1) * deep]
            lay(block, places(zn, notes, per, 0, per - 1), start, False)

        @pl.when(flag_ref[0] != 0)
        def _():
            @pl.loop(0, few)
            def _(k):
                pair = g * few + k
                top = pl.multiple_of(k * deep, 16)
                ends = [in_ref[pl.ds(pl.multiple_of(top + (h + 1) * per - 16, 16), 16), 0:128] for h in (0, 1)]
                notes = [e.astype(F32)[15:16] for e in ends]
                start = pl.multiple_of(pair * pad, 16)
                from_row = pl.multiple_of(pair * more_deep, 16)
                pltpu.sync_copy(more_ref.at[pl.ds(from_row, more_deep), :], more_vmem)
                lay(more_vmem[...], places(zn, notes, rest, per - 1, rest), start, True)

    @pl.when(g >= steps)
    def _():
        first = (g - steps) * slots
        logits = []
        for k in range(slots):
            panel = panel_ref[k]
            wide = panel.astype(F32)
            sqnorm = jnp.sum(wide * wide, axis=1, keepdims=True)
            logits.append(dot(panel, held[first + k][:, :width], ((1,), (1,))) - 0.5 * sqnorm)
        for k in range(slots):
            peak = jnp.max(logits[k], axis=0, keepdims=True)
            shifted = jnp.exp(logits[k] - peak)
            total = jnp.sum(shifted, axis=0, keepdims=True)
            score_ref[pl.ds(first + k, 1), :] = peak + jnp.log(total)
            weights = (shifted * (1.0 / total)).astype(BF)
            sums = dot(weights, held[first + k])
            sums_ref[k] = sums[:, :width].astype(BF)
            mass_ref[pl.ds(first + k, 1), :] = jnp.transpose(sums[:, width:])[0:1]


def assign(flag, rows, more, panels, pairs, few=8, slots=2):
    zn, fine, width = panels.shape
    deep, more_deep = rows.shape[0] // pairs, more.shape[0] // pairs
    spread = pairs * 2 * CAP
    steps = pairs // few
    whole = lambda g, f: (0, 0)
    by_slot = lambda g, f: (jnp.maximum(g - steps, 0), 0, 0)
    return pl.pallas_call(
        functools.partial(assign_kernel, steps, zn, few, slots),
        grid_spec=pltpu.PrefetchScalarGridSpec(
            num_scalar_prefetch=1,
            grid=(steps + zn // slots,),
            in_specs=[
                pl.BlockSpec((few * deep, width), lambda g, f: (jnp.minimum(g, steps - 1), 0)),
                pl.BlockSpec(memory_space=pl.ANY),
                pl.BlockSpec((slots, fine, width), by_slot),
            ],
            out_specs=[
                pl.BlockSpec((slots, fine, width), by_slot),
                pl.BlockSpec((zn, fine), whole),
                pl.BlockSpec((zn, spread), whole),
            ],
            scratch_shapes=[
                pltpu.VMEM((zn, spread, width + 128), BF),
                pltpu.VMEM((more_deep, width), BF),
            ],
        ),
        out_shape=(
            jax.ShapeDtypeStruct((zn, fine, width), BF),
            jax.ShapeDtypeStruct((zn, fine), F32),
            jax.ShapeDtypeStruct((zn, spread), F32),
        ),
        cost_estimate=pl.CostEstimate(
            flops=8 * 10**9, bytes_accessed=2 * 10**7, transcendentals=2 * 10**6
        ),
        name="assign",
    )(flag, rows, more, panels)


def lookup_kernel(place_ref, table_ref, out_ref):
    slots, rows = table_ref.shape[1], place_ref.shape[1]
    table = table_ref[...]
    hi = table.astype(BF)
    rest = table - hi.astype(F32)
    mid = rest.astype(BF)
    low = (rest - mid.astype(F32)).astype(BF)
    hot = onehot(iota((slots, rows), 0) == place_ref[1:2, :])
    value = dot(hi, hot) + dot(mid, hot) + dot(low, hot)
    mine = iota(value.shape, 0) == place_ref[2:3, :]
    out_ref[...] = jnp.sum(jnp.where(mine, value, 0.0), axis=0, keepdims=True)


def lookup(place, table):
    return pl.pallas_call(
        lookup_kernel,
        out_shape=jax.ShapeDtypeStruct((1, place.shape[1]), F32),
        cost_estimate=pl.CostEstimate(flops=10**8, bytes_accessed=10**5, transcendentals=0),
        name="lookup",
    )(place, table)


def exchange(x, axes):
    return lax.all_to_all(x, axes, split_axis=0, concat_axis=0, tiled=True)


def local(points, coarse_id, owner_map, centroids):
    zn, cores = lax.axis_size("z"), lax.axis_size("core")
    dpn = lax.axis_size("y") * lax.axis_size("x")
    peers = dpn * cores
    bound = zn * CAP
    rows, width = points.shape

    panel = exchange(centroids, ("y", "x")).reshape(-1, width)
    place, note = index(
        coarse_id.reshape(1, rows), owner_map.reshape(1, -1), zn, dpn, cores, bound
    )
    packed = pack(place, points, note, ROWS, 0, bound, 1024, True)
    arrived = exchange(packed.reshape(peers, ROWS, width), PLANE)
    panels = lax.all_gather(panel, "z", axis=0)

    most = jnp.max(arrived[:, ROWS - 1, zn].astype(F32))

    def second(per):
        block = pack(place, points, note, per, ROWS - 1, bound, 16 * per, False)
        block = exchange(block.reshape(peers, per, width), PLANE)
        return jnp.pad(block, ((0, 0), (0, REST - per), (0, 0))).reshape(peers * REST, width)

    level = (most > ROWS - 1).astype(jnp.int32) + (most > ROWS - 1 + SOME).astype(jnp.int32)
    more = lax.switch(
        level,
        (lambda: jnp.zeros((peers * REST, width), BF), lambda: second(SOME), lambda: second(REST)),
    )
    sums, mass, score = assign(
        level.reshape(1), arrived.reshape(peers * ROWS, width), more, panels, peers // 2
    )
    sums = lax.psum_scatter(sums, "z", scatter_dimension=0, tiled=True)[0]
    score = score.reshape(zn, peers, CAP).transpose(1, 0, 2).reshape(peers, zn * CAP)
    score = exchange(score, PLANE).reshape(peers * zn, CAP).T
    point_score = lookup(place, score).reshape(rows)
    mass = jnp.sum(exchange(mass, "z"), axis=0)
    updated = (sums.astype(F32) + PRIOR * panel.astype(F32)) / (mass[:, None] + PRIOR)
    updated = updated.astype(BF).reshape(dpn, -1, width)
    return exchange(updated, ("y", "x")), point_score


def solution(mesh):
    devices = mesh.devices
    chips = Mesh(devices.reshape(4, 4, 8, 2), ("y", "x", "z", "core"))
    every = ("y", "x", "z", "core")
    grid = P(("z", "core"), ("y", "x"), None)
    return jax.shard_map(
        local,
        mesh=chips,
        in_specs=(P(every, None), P(every, None), P(), grid),
        out_specs=(grid, P(every)),
        check_vma=False,
    )
```

```python
import functools
import jax
import jax.numpy as jnp
from jax import lax
from jax.experimental import pallas as pl
from jax.experimental.pallas import tpu as pltpu
from jax.sharding import Mesh, PartitionSpec as P

PRIOR = 4.0
CAP = 24
ROWS = 128
BLOCK = 256
WINDOW = 64
SOME, REST = 16, 72
PLANE = ("y", "x", "core")
BF = jnp.bfloat16
F32 = jnp.float32


def iota(shape, dim):
    return lax.broadcasted_iota(jnp.int32, shape, dim)


def dot(a, b, dims=((1,), (0,))):
    return lax.dot_general(a, b, (dims, ((), ())), preferred_element_type=F32)


def onehot(mask):
    return jnp.where(mask, 1.0, 0.0).astype(BF)


def index_kernel(
    zn, dpn, cores, bound, coarse_ref, owner_ref, place_ref, note_ref, segment_ref, hot_ref
):
    slots = owner_ref.shape[1]
    rows = coarse_ref.shape[1]
    blocks = rows // BLOCK
    peers, width = note_ref.shape
    owner = owner_ref[...]
    column, cluster = owner % dpn, owner // dpn
    lane_of = (column * cores + cluster % cores) * zn + cluster // cores
    move = onehot(iota((slots, slots), 0) == lane_of)
    earlier = onehot(iota((BLOCK, BLOCK), 0) < iota((BLOCK, BLOCK), 1))
    ranks, sizes = [], []
    for b in range(blocks):
        part = slice(b * BLOCK, (b + 1) * BLOCK)
        named = onehot(iota((slots, BLOCK), 0) == coarse_ref[:, part])
        hot = dot(move, named)
        hot_bf = hot.astype(BF)
        hot_ref[:, part] = hot_bf
        ranks.append(jnp.sum(hot * dot(hot_bf, earlier), axis=0, keepdims=True))
        sizes.append(dot(jnp.ones((8, BLOCK), BF), hot_bf, ((1,), (1,)))[0:1])
    rank = jnp.concatenate(ranks, axis=1)
    size = jnp.concatenate(sizes, axis=0)
    done, carry = jnp.zeros((1, slots), F32), []
    for b in range(blocks):
        carry.append(done)
        done = done + sizes[b]
    carry = jnp.concatenate(carry, axis=0)
    la, lb = iota((slots, slots), 0), iota((slots, slots), 1)
    lower = dot(size.astype(BF), onehot(la < lb))
    group = onehot((la // zn == lb // zn) & (la < lb))
    offset = dot(jnp.broadcast_to(done, (8, slots)).astype(BF), group)
    which = iota((8, slots), 0)
    query = jnp.where(which == 0, offset, iota((8, slots), 1).astype(F32))
    query = jnp.concatenate([query, lower, carry], axis=0).astype(BF)
    found = dot(query, hot_ref[...])
    own = iota((blocks, rows), 1) // BLOCK == iota((blocks, rows), 0)
    mine = lambda k: jnp.sum(
        jnp.where(own, found[8 + k * blocks : 8 + (k + 1) * blocks], 0.0), axis=0, keepdims=True
    )
    sort = (rank + mine(0)).astype(jnp.int32)
    rank = (rank + mine(1)).astype(jnp.int32)
    lane = found[1:2].astype(jnp.int32)
    pos = (lane // zn) * bound + found[0:1].astype(jnp.int32) + rank
    row = iota((8, rows), 0)
    place_ref[...] = jnp.where(
        row == 0, pos, jnp.where(row == 1, lane, jnp.where(row == 2, rank, sort))
    )
    segment_ref[:, :slots] = lower.astype(jnp.int32)
    segment_ref[:, slots:] = jnp.full((blocks, 128), BLOCK, jnp.int32)
    mine = iota((peers, slots), 1) // zn == iota((peers, slots), 0)
    spread = jnp.where(mine, done, 0.0)
    most = jnp.max(jnp.sum(spread, axis=1, keepdims=True), axis=0, keepdims=True)
    spot = onehot(iota((slots, width), 0) % zn == iota((slots, width), 1))
    note = dot(spread.astype(BF), spot)
    note_ref[...] = jnp.where(iota((peers, width), 1) == zn, most, note)


def index(coarse, owner, zn, dpn, cores, bound):
    rows, slots = coarse.shape[1], owner.shape[1]
    return pl.pallas_call(
        functools.partial(index_kernel, zn, dpn, cores, bound),
        out_shape=(
            jax.ShapeDtypeStruct((8, rows), jnp.int32),
            jax.ShapeDtypeStruct((dpn * cores, 128), F32),
            jax.ShapeDtypeStruct((rows // BLOCK, slots + 128), jnp.int32),
        ),
        scratch_shapes=[pltpu.VMEM((slots, rows), BF)],
        cost_estimate=pl.CostEstimate(flops=10**9, bytes_accessed=10**5, transcendentals=0),
        name="place",
    )(coarse, owner)


def pack_kernel(per, first, bound, place_ref, points_ref, out_ref):
    g = pl.program_id(0)
    tall = out_ref.shape[0]
    i = iota((tall, 1), 0)
    want = (g * (tall // per) + i // per) * bound + first + i % per
    pick = onehot(place_ref[0:1, :] == want)
    out_ref[...] = dot(pick, points_ref[...]).astype(BF)


def pack(place, points, peers, per, first, bound, tall):
    rows, width = points.shape
    return pl.pallas_call(
        functools.partial(pack_kernel, per, first, bound),
        grid=(peers * per // tall,),
        in_specs=[
            pl.BlockSpec((8, rows), lambda g: (0, 0)),
            pl.BlockSpec((rows, width), lambda g: (0, 0)),
        ],
        out_specs=pl.BlockSpec((tall, width), lambda g: (g, 0)),
        out_shape=jax.ShapeDtypeStruct((peers * per, width), BF),
        cost_estimate=pl.CostEstimate(
            flops=2 * peers * per * rows * width, bytes_accessed=10**7, transcendentals=0
        ),
        name="pack",
    )(place, points)


def sort_pack_kernel(
    per, bound, zn, segment_ref, place_ref, points_ref, note_ref, out_ref, sorted_ref, key_ref,
    near_ref,
):
    g = pl.program_id(0)
    tall = out_ref.shape[0]
    blocks = points_ref.shape[0] // BLOCK
    wide = BLOCK // WINDOW

    @pl.when(g == 0)
    def _():
        for b in range(blocks):
            part = slice(b * BLOCK, (b + 1) * BLOCK)
            move = onehot(iota((BLOCK, BLOCK), 0) == place_ref[3:4, part])
            sorted_ref[part] = dot(move, points_ref[part]).astype(BF)
            key = place_ref[0:1, part]
            which = iota((8, BLOCK), 0)
            halves = jnp.where(which == 0, key // 128, jnp.where(which == 1, key % 128, 0))
            keys = dot(halves.astype(F32).astype(BF), move, ((1,), (1,)))
            key_ref[b : b + 1, :] = (keys[0:1] * 128.0 + keys[1:2]).astype(jnp.int32)

    both = 2 * per
    i = iota((both, 1), 0)
    lane = iota((1, BLOCK), 1)

    def picked(q, group, starts, news):
        want = (group * 2 + i // per) * bound + i % per
        keys = []
        for b in range(blocks):
            rows = pl.multiple_of(b * BLOCK + starts[b], 16)
            near_ref[q, b * WINDOW : (b + 1) * WINDOW, :] = sorted_ref[pl.ds(rows, WINDOW), :]
            key = key_ref[b : b + 1, :]
            if news is not None:
                key = jnp.where(lane >= news[b], key, -1)
            shift = (b % wide) * WINDOW + BLOCK - starts[b]
            key = pltpu.roll(key, shift % BLOCK, 1)
            if b % wide == 0:
                keys.append(key)
            else:
                keys[-1] = jnp.where(lane >= (b % wide) * WINDOW, key, keys[-1])
        pick = onehot(jnp.concatenate(keys, axis=1) == want)
        return dot(pick, near_ref[q])

    groups = tall // both
    longest, lows_of = jnp.int32(0), []
    for q in range(groups):
        first = (g * groups + q) * 2 * zn
        lows = [segment_ref[b, first] // 16 * 16 for b in range(blocks)]
        highs = [segment_ref[b, first + 2 * zn] for b in range(blocks)]
        for low, high in zip(lows, highs):
            longest = jnp.maximum(longest, high - low)
        lows_of.append(lows)
        starts = [jnp.minimum(low, BLOCK - WINDOW) for low in lows]
        out_ref[q * both : (q + 1) * both] = picked(q, g * groups + q, starts, None).astype(BF)

    @pl.when(longest > WINDOW)
    def _():
        @pl.loop(1, (longest + WINDOW - 1) // WINDOW)
        def _(w):
            for q in range(groups):
                here = slice(q * both, (q + 1) * both)
                news = [low + w * WINDOW for low in lows_of[q]]
                starts = [jnp.minimum(new, BLOCK - WINDOW) for new in news]
                more = picked(q, g * groups + q, starts, news)
                out_ref[here] = (out_ref[here].astype(F32) + more).astype(BF)

    for k in range(tall // per):
        tile = slice((k + 1) * per - 16, (k + 1) * per)
        note = jnp.broadcast_to(note_ref[k : k + 1], (16, 128))
        end = iota((16, 128), 0) == 15
        out_ref[tile, :128] = jnp.where(end, note, out_ref[tile, :128].astype(F32)).astype(BF)


def sort_pack(segment, place, points, note, per, bound, zn, tall):
    rows, width = points.shape
    peers = note.shape[0]
    blocks = rows // BLOCK
    return pl.pallas_call(
        functools.partial(sort_pack_kernel, per, bound, zn),
        grid_spec=pltpu.PrefetchScalarGridSpec(
            num_scalar_prefetch=1,
            grid=(peers * per // tall,),
            in_specs=[
                pl.BlockSpec((8, rows), lambda g, s: (0, 0)),
                pl.BlockSpec((rows, width), lambda g, s: (0, 0)),
                pl.BlockSpec((tall // per, 128), lambda g, s: (g, 0)),
            ],
            out_specs=pl.BlockSpec((tall, width), lambda g, s: (g, 0)),
            scratch_shapes=[
                pltpu.VMEM((rows, width), BF),
                pltpu.VMEM((blocks, BLOCK), jnp.int32),
                pltpu.VMEM((tall // (2 * per), blocks * WINDOW, width), BF),
            ],
        ),
        out_shape=jax.ShapeDtypeStruct((peers * per, width), BF),
        cost_estimate=pl.CostEstimate(
            flops=5 * 10**9, bytes_accessed=10**7, transcendentals=0
        ),
        name="sort_pack",
    )(segment, place, points, note)


def places(zn, notes, per, first, count):
    lane, sub = iota((zn, 128), 1), iota((zn, 128), 0)
    sides = []
    for note in notes:
        note = jnp.broadcast_to(note, (zn, 128))
        ends = jnp.sum(jnp.where(lane <= sub, note, 0.0), axis=1, keepdims=True)
        size = jnp.sum(jnp.where(lane == sub, note, 0.0), axis=1, keepdims=True)
        sides.append((ends, size))
    c = iota((zn, 2 * per), 1)
    second = c >= per
    at = c - jnp.where(second, per, 0)
    pos = (at + first).astype(F32)
    passed = pos >= jnp.where(second, sides[1][0], sides[0][0])
    size = jnp.where(second, sides[1][1], sides[0][1])
    slot = jnp.sum(jnp.where(passed, 1.0, 0.0), axis=0, keepdims=True)
    begin = jnp.sum(jnp.where(passed, size, 0.0), axis=0, keepdims=True)
    side = jnp.where(second[0:1], 1.0 * CAP, 0.0)
    dest = slot * (2 * CAP) + side + pos[0:1] - begin
    return jnp.where(at[0:1] < count, dest, -1.0).astype(jnp.int32)


def assign_kernel(
    steps, zn, few, slots, flag_ref, in_ref, more_ref, panel_ref, sums_ref, mass_ref, score_ref,
    held, more_vmem,
):
    g = pl.program_id(0)
    pad = 2 * CAP
    tall = zn * pad
    width = in_ref.shape[1]
    deep, more_deep = in_ref.shape[0] // few, more_vmem.shape[0] // (steps * few)
    per, rest = deep // 2, more_deep // 2

    def lay(block, dest, start, add):
        pick = jnp.where(iota((tall, block.shape[0]), 0) == dest, 1.0, 0.0)
        there = jnp.broadcast_to(jnp.sum(pick, axis=1, keepdims=True), (tall, 128))
        laid = dot(pick.astype(BF), block)
        for j in range(zn):
            part = slice(j * pad, (j + 1) * pad)
            for value, lanes in ((laid[part], slice(0, width)), (there[part], slice(width, width + 128))):
                if add:
                    value = value + held[j, pl.ds(start, pad), lanes].astype(F32)
                held[j, pl.ds(start, pad), lanes] = value.astype(BF)

    @pl.when(g < steps)
    def _():
        for k in range(few):
            last = [k * deep + per - 1, (k + 1) * deep - 1]
            notes = [in_ref[r : r + 1, 0:128].astype(F32) for r in last]
            start = pl.multiple_of((g * few + k) * pad, 16)
            block = in_ref[k * deep : (k + 1) * deep]
            lay(block, places(zn, notes, per, 0, per - 1), start, False)

        @pl.when(flag_ref[0] != 0)
        def _():
            @pl.when(g == 0)
            def _():
                pltpu.sync_copy(more_ref, more_vmem)

            @pl.loop(0, few)
            def _(k):
                pair = g * few + k
                top = pl.multiple_of(k * deep, 16)
                ends = [in_ref[pl.ds(pl.multiple_of(top + (h + 1) * per - 16, 16), 16), 0:128] for h in (0, 1)]
                notes = [e.astype(F32)[15:16] for e in ends]
                start = pl.multiple_of(pair * pad, 16)
                from_row = pl.multiple_of(pair * more_deep, 16)
                lay(more_vmem[pl.ds(from_row, more_deep), :], places(zn, notes, rest, per - 1, rest), start, True)

    @pl.when(g >= steps)
    def _():
        first = (g - steps) * slots
        logits = []
        for k in range(slots):
            panel = panel_ref[k]
            wide = panel.astype(F32)
            sqnorm = jnp.sum(wide * wide, axis=1, keepdims=True)
            logits.append(dot(panel, held[first + k][:, :width], ((1,), (1,))) - 0.5 * sqnorm)
        for k in range(slots):
            peak = jnp.max(logits[k], axis=0, keepdims=True)
            shifted = jnp.exp(logits[k] - peak)
            total = jnp.sum(shifted, axis=0, keepdims=True)
            score_ref[pl.ds(first + k, 1), :] = peak + jnp.log(total)
            weights = (shifted * (1.0 / total)).astype(BF)
            sums = dot(weights, held[first + k])
            sums_ref[k] = sums[:, :width].astype(BF)
            mass_ref[pl.ds(first + k, 1), :] = jnp.transpose(sums[:, width:])[0:1]


def assign(flag, rows, more, panels, pairs, few=8, slots=2):
    zn, fine, width = panels.shape
    deep = rows.shape[0] // pairs
    spread = pairs * 2 * CAP
    steps = pairs // few
    whole = lambda g, f: (0, 0)
    by_slot = lambda g, f: (jnp.maximum(g - steps, 0), 0, 0)
    return pl.pallas_call(
        functools.partial(assign_kernel, steps, zn, few, slots),
        grid_spec=pltpu.PrefetchScalarGridSpec(
            num_scalar_prefetch=1,
            grid=(steps + zn // slots,),
            in_specs=[
                pl.BlockSpec((few * deep, width), lambda g, f: (jnp.minimum(g, steps - 1), 0)),
                pl.BlockSpec(memory_space=pl.ANY),
                pl.BlockSpec((slots, fine, width), by_slot),
            ],
            out_specs=[
                pl.BlockSpec((slots, fine, width), by_slot),
                pl.BlockSpec((zn, fine), whole),
                pl.BlockSpec((zn, spread), whole),
            ],
            scratch_shapes=[
                pltpu.VMEM((zn, spread, width + 128), BF),
                pltpu.VMEM(more.shape, BF),
            ],
        ),
        out_shape=(
            jax.ShapeDtypeStruct((zn, fine, width), BF),
            jax.ShapeDtypeStruct((zn, fine), F32),
            jax.ShapeDtypeStruct((zn, spread), F32),
        ),
        cost_estimate=pl.CostEstimate(
            flops=8 * 10**9, bytes_accessed=2 * 10**7, transcendentals=2 * 10**6
        ),
        name="assign",
    )(flag, rows, more, panels)


def lookup_kernel(place_ref, table_ref, out_ref):
    slots, rows = table_ref.shape[1], place_ref.shape[1]
    table = table_ref[...]
    hi = table.astype(BF)
    rest = table - hi.astype(F32)
    mid = rest.astype(BF)
    low = (rest - mid.astype(F32)).astype(BF)
    hot = onehot(iota((slots, rows), 0) == place_ref[1:2, :])
    value = dot(hi, hot) + dot(mid, hot) + dot(low, hot)
    mine = iota(value.shape, 0) == place_ref[2:3, :]
    out_ref[...] = jnp.sum(jnp.where(mine, value, 0.0), axis=0, keepdims=True)


def lookup(place, table):
    return pl.pallas_call(
        lookup_kernel,
        out_shape=jax.ShapeDtypeStruct((1, place.shape[1]), F32),
        cost_estimate=pl.CostEstimate(flops=10**8, bytes_accessed=10**5, transcendentals=0),
        name="lookup",
    )(place, table)


def exchange(x, axes):
    return lax.all_to_all(x, axes, split_axis=0, concat_axis=0, tiled=True)


def local(points, coarse_id, owner_map, centroids):
    zn, cores = lax.axis_size("z"), lax.axis_size("core")
    dpn = lax.axis_size("y") * lax.axis_size("x")
    peers = dpn * cores
    bound = zn * CAP
    rows, width = points.shape

    panel = exchange(centroids, ("y", "x")).reshape(-1, width)
    place, note, segment = index(
        coarse_id.reshape(1, rows), owner_map.reshape(1, -1), zn, dpn, cores, bound
    )
    packed = sort_pack(segment, place, points, note, ROWS, bound, zn, 1024)
    arrived = exchange(packed.reshape(peers, ROWS, width), PLANE)
    panels = lax.all_gather(panel, "z", axis=0)

    most = jnp.max(arrived[:, ROWS - 1, zn].astype(F32))

    def second(per):
        block = pack(place, points, peers, per, ROWS - 1, bound, 16 * per)
        block = exchange(block.reshape(peers, per, width), PLANE)
        return jnp.pad(block, ((0, 0), (0, REST - per), (0, 0))).reshape(peers * REST, width)

    level = (most > ROWS - 1).astype(jnp.int32) + (most > ROWS - 1 + SOME).astype(jnp.int32)
    more = lax.switch(
        level,
        (lambda: jnp.zeros((peers * REST, width), BF), lambda: second(SOME), lambda: second(REST)),
    )
    sums, mass, score = assign(
        level.reshape(1), arrived.reshape(peers * ROWS, width), more, panels, peers // 2
    )
    sums = lax.psum_scatter(sums, "z", scatter_dimension=0, tiled=True)[0]
    score = score.reshape(zn, peers, CAP).transpose(1, 0, 2).reshape(peers, zn * CAP)
    score = exchange(score, PLANE).reshape(peers * zn, CAP).T
    point_score = lookup(place, score).reshape(rows)
    mass = jnp.sum(exchange(mass, "z"), axis=0)
    updated = (sums.astype(F32) + PRIOR * panel.astype(F32)) / (mass[:, None] + PRIOR)
    updated = updated.astype(BF).reshape(dpn, -1, width)
    return exchange(updated, ("y", "x")), point_score


def solution(mesh):
    devices = mesh.devices
    chips = Mesh(devices.reshape(4, 4, 8, 2), ("y", "x", "z", "core"))
    every = ("y", "x", "z", "core")
    grid = P(("z", "core"), ("y", "x"), None)
    return jax.shard_map(
        local,
        mesh=chips,
        in_specs=(P(every, None), P(every, None), P(), grid),
        out_specs=(grid, P(every)),
        check_vma=False,
    )
```

```python
import functools
import jax
import jax.numpy as jnp
from jax import lax
from jax.experimental import pallas as pl
from jax.experimental.pallas import tpu as pltpu
from jax.sharding import Mesh, PartitionSpec as P

PRIOR = 4.0
CAP = 24
ROWS = 128
BLOCK = 256
WINDOW = 64
SOME, REST = 16, 72
PLANE = ("y", "x", "core")
BF = jnp.bfloat16
F32 = jnp.float32


def iota(shape, dim):
    return lax.broadcasted_iota(jnp.int32, shape, dim)


def dot(a, b, dims=((1,), (0,))):
    return lax.dot_general(a, b, (dims, ((), ())), preferred_element_type=F32)


def onehot(mask):
    return jnp.where(mask, 1.0, 0.0).astype(BF)


def index_kernel(
    zn, dpn, cores, bound, coarse_ref, owner_ref, place_ref, note_ref, segment_ref, hot_ref
):
    slots = owner_ref.shape[1]
    rows = coarse_ref.shape[1]
    blocks = rows // BLOCK
    peers, width = note_ref.shape
    owner = owner_ref[...]
    column, cluster = owner % dpn, owner // dpn
    lane_of = (column * cores + cluster % cores) * zn + cluster // cores
    move = onehot(iota((slots, slots), 0) == lane_of)
    earlier = onehot(iota((BLOCK, BLOCK), 0) < iota((BLOCK, BLOCK), 1))
    ranks, sizes = [], []
    for b in range(blocks):
        part = slice(b * BLOCK, (b + 1) * BLOCK)
        named = onehot(iota((slots, BLOCK), 0) == coarse_ref[:, part])
        hot = dot(move, named)
        hot_bf = hot.astype(BF)
        hot_ref[:, part] = hot_bf
        ranks.append(jnp.sum(hot * dot(hot_bf, earlier), axis=0, keepdims=True))
        sizes.append(dot(jnp.ones((8, BLOCK), BF), hot_bf, ((1,), (1,)))[0:1])
    rank = jnp.concatenate(ranks, axis=1)
    size = jnp.concatenate(sizes, axis=0)
    done, carry = jnp.zeros((1, slots), F32), []
    for b in range(blocks):
        carry.append(done)
        done = done + sizes[b]
    carry = jnp.concatenate(carry, axis=0)
    la, lb = iota((slots, slots), 0), iota((slots, slots), 1)
    lower = dot(size.astype(BF), onehot(la < lb))
    group = onehot((la // zn == lb // zn) & (la < lb))
    offset = dot(jnp.broadcast_to(done, (8, slots)).astype(BF), group)
    which = iota((8, slots), 0)
    query = jnp.where(which == 0, offset, iota((8, slots), 1).astype(F32))
    query = jnp.concatenate([query, lower, carry], axis=0).astype(BF)
    found = dot(query, hot_ref[...])
    own = iota((blocks, rows), 1) // BLOCK == iota((blocks, rows), 0)
    mine = lambda k: jnp.sum(
        jnp.where(own, found[8 + k * blocks : 8 + (k + 1) * blocks], 0.0), axis=0, keepdims=True
    )
    sort = (rank + mine(0)).astype(jnp.int32)
    rank = (rank + mine(1)).astype(jnp.int32)
    lane = found[1:2].astype(jnp.int32)
    pos = (lane // zn) * bound + found[0:1].astype(jnp.int32) + rank
    row = iota((8, rows), 0)
    place_ref[...] = jnp.where(
        row == 0, pos, jnp.where(row == 1, lane, jnp.where(row == 2, rank, sort))
    )
    segment_ref[:, :slots] = lower.astype(jnp.int32)
    segment_ref[:, slots:] = jnp.full((blocks, 128), BLOCK, jnp.int32)
    mine = iota((peers, slots), 1) // zn == iota((peers, slots), 0)
    spread = jnp.where(mine, done, 0.0)
    most = jnp.max(jnp.sum(spread, axis=1, keepdims=True), axis=0, keepdims=True)
    spot = onehot(iota((slots, width), 0) % zn == iota((slots, width), 1))
    note = dot(spread.astype(BF), spot)
    note_ref[...] = jnp.where(iota((peers, width), 1) == zn, most, note)


def index(coarse, owner, zn, dpn, cores, bound):
    rows, slots = coarse.shape[1], owner.shape[1]
    return pl.pallas_call(
        functools.partial(index_kernel, zn, dpn, cores, bound),
        out_shape=(
            jax.ShapeDtypeStruct((8, rows), jnp.int32),
            jax.ShapeDtypeStruct((dpn * cores, 128), F32),
            jax.ShapeDtypeStruct((rows // BLOCK, slots + 128), jnp.int32),
        ),
        scratch_shapes=[pltpu.VMEM((slots, rows), BF)],
        cost_estimate=pl.CostEstimate(flops=10**9, bytes_accessed=10**5, transcendentals=0),
        name="place",
    )(coarse, owner)


def pack_kernel(per, first, bound, place_ref, points_ref, out_ref):
    g = pl.program_id(0)
    tall = out_ref.shape[0]
    i = iota((tall, 1), 0)
    want = (g * (tall // per) + i // per) * bound + first + i % per
    pick = onehot(place_ref[0:1, :] == want)
    out_ref[...] = dot(pick, points_ref[...]).astype(BF)


def pack(place, points, peers, per, first, bound, tall):
    rows, width = points.shape
    return pl.pallas_call(
        functools.partial(pack_kernel, per, first, bound),
        grid=(peers * per // tall,),
        in_specs=[
            pl.BlockSpec((8, rows), lambda g: (0, 0)),
            pl.BlockSpec((rows, width), lambda g: (0, 0)),
        ],
        out_specs=pl.BlockSpec((tall, width), lambda g: (g, 0)),
        out_shape=jax.ShapeDtypeStruct((peers * per, width), BF),
        cost_estimate=pl.CostEstimate(
            flops=2 * peers * per * rows * width, bytes_accessed=10**7, transcendentals=0
        ),
        name="pack",
    )(place, points)


def sort_pack_kernel(
    per, bound, zn, segment_ref, place_ref, points_ref, note_ref, out_ref, sorted_ref, key_ref,
    near_ref,
):
    g = pl.program_id(0)
    tall = out_ref.shape[0]
    blocks = points_ref.shape[0] // BLOCK
    wide = BLOCK // WINDOW

    @pl.when(g == 0)
    def _():
        for b in range(blocks):
            part = slice(b * BLOCK, (b + 1) * BLOCK)
            move = onehot(iota((BLOCK, BLOCK), 0) == place_ref[3:4, part])
            sorted_ref[part] = dot(move, points_ref[part]).astype(BF)
            key = place_ref[0:1, part]
            which = iota((8, BLOCK), 0)
            halves = jnp.where(which == 0, key // 128, jnp.where(which == 1, key % 128, 0))
            keys = dot(halves.astype(F32).astype(BF), move, ((1,), (1,)))
            key_ref[b : b + 1, :] = (keys[0:1] * 128.0 + keys[1:2]).astype(jnp.int32)

    both = 2 * per
    i = iota((both, 1), 0)
    lane = iota((1, BLOCK), 1)

    def picked(q, group, starts, news):
        want = (group * 2 + i // per) * bound + i % per
        keys = []
        for b in range(blocks):
            rows = pl.multiple_of(b * BLOCK + starts[b], 16)
            near_ref[q, b * WINDOW : (b + 1) * WINDOW, :] = sorted_ref[pl.ds(rows, WINDOW), :]
            key = key_ref[b : b + 1, :]
            if news is not None:
                key = jnp.where(lane >= news[b], key, -1)
            shift = (b % wide) * WINDOW + BLOCK - starts[b]
            key = pltpu.roll(key, shift % BLOCK, 1)
            if b % wide == 0:
                keys.append(key)
            else:
                keys[-1] = jnp.where(lane >= (b % wide) * WINDOW, key, keys[-1])
        pick = onehot(jnp.concatenate(keys, axis=1) == want)
        return dot(pick, near_ref[q])

    groups = tall // both
    longest, lows_of = jnp.int32(0), []
    for q in range(groups):
        first = (g * groups + q) * 2 * zn
        lows = [segment_ref[b, first] // 16 * 16 for b in range(blocks)]
        highs = [segment_ref[b, first + 2 * zn] for b in range(blocks)]
        for low, high in zip(lows, highs):
            longest = jnp.maximum(longest, high - low)
        lows_of.append(lows)
        starts = [jnp.minimum(low, BLOCK - WINDOW) for low in lows]
        out_ref[q * both : (q + 1) * both] = picked(q, g * groups + q, starts, None).astype(BF)

    @pl.when(longest > WINDOW)
    def _():
        @pl.loop(1, (longest + WINDOW - 1) // WINDOW)
        def _(w):
            for q in range(groups):
                here = slice(q * both, (q + 1) * both)
                news = [low + w * WINDOW for low in lows_of[q]]
                starts = [jnp.minimum(new, BLOCK - WINDOW) for new in news]
                more = picked(q, g * groups + q, starts, news)
                out_ref[here] = (out_ref[here].astype(F32) + more).astype(BF)

    for k in range(tall // per):
        tile = slice((k + 1) * per - 16, (k + 1) * per)
        note = jnp.broadcast_to(note_ref[k : k + 1], (16, 128))
        end = iota((16, 128), 0) == 15
        out_ref[tile, :128] = jnp.where(end, note, out_ref[tile, :128].astype(F32)).astype(BF)


def sort_pack(segment, place, points, note, per, bound, zn, tall):
    rows, width = points.shape
    peers = note.shape[0]
    blocks = rows // BLOCK
    return pl.pallas_call(
        functools.partial(sort_pack_kernel, per, bound, zn),
        grid_spec=pltpu.PrefetchScalarGridSpec(
            num_scalar_prefetch=1,
            grid=(peers * per // tall,),
            in_specs=[
                pl.BlockSpec((8, rows), lambda g, s: (0, 0)),
                pl.BlockSpec((rows, width), lambda g, s: (0, 0)),
                pl.BlockSpec((tall // per, 128), lambda g, s: (g, 0)),
            ],
            out_specs=pl.BlockSpec((tall, width), lambda g, s: (g, 0)),
            scratch_shapes=[
                pltpu.VMEM((rows, width), BF),
                pltpu.VMEM((blocks, BLOCK), jnp.int32),
                pltpu.VMEM((tall // (2 * per), blocks * WINDOW, width), BF),
            ],
        ),
        out_shape=jax.ShapeDtypeStruct((peers * per, width), BF),
        cost_estimate=pl.CostEstimate(
            flops=5 * 10**9, bytes_accessed=10**7, transcendentals=0
        ),
        name="sort_pack",
    )(segment, place, points, note)


def places(zn, notes, per, first, count):
    lane, sub = iota((zn, 128), 1), iota((zn, 128), 0)
    sides = []
    for note in notes:
        note = jnp.broadcast_to(note, (zn, 128))
        ends = jnp.sum(jnp.where(lane <= sub, note, 0.0), axis=1, keepdims=True)
        size = jnp.sum(jnp.where(lane == sub, note, 0.0), axis=1, keepdims=True)
        sides.append((ends, size))
    c = iota((zn, 2 * per), 1)
    second = c >= per
    at = c - jnp.where(second, per, 0)
    pos = (at + first).astype(F32)
    passed = pos >= jnp.where(second, sides[1][0], sides[0][0])
    size = jnp.where(second, sides[1][1], sides[0][1])
    slot = jnp.sum(jnp.where(passed, 1.0, 0.0), axis=0, keepdims=True)
    begin = jnp.sum(jnp.where(passed, size, 0.0), axis=0, keepdims=True)
    side = jnp.where(second[0:1], 1.0 * CAP, 0.0)
    dest = slot * (2 * CAP) + side + pos[0:1] - begin
    return jnp.where(at[0:1] < count, dest, -1.0).astype(jnp.int32)


def assign_kernel(
    steps, zn, few, slots, flag_ref, in_ref, more_ref, panel_ref, sums_ref, mass_ref, score_ref,
    held, more_vmem,
):
    g = pl.program_id(0)
    pad = 2 * CAP
    tall = zn * pad
    width = in_ref.shape[1]
    deep, more_deep = in_ref.shape[0] // few, more_vmem.shape[0] // (steps * few)
    per, rest = deep // 2, more_deep // 2

    def lay(block, dest, start, add):
        pick = jnp.where(iota((tall, block.shape[0]), 0) == dest, 1.0, 0.0)
        there = jnp.broadcast_to(jnp.sum(pick, axis=1, keepdims=True), (tall, 128))
        laid = dot(pick.astype(BF), block)
        for j in range(zn):
            part = slice(j * pad, (j + 1) * pad)
            for value, lanes in ((laid[part], slice(0, width)), (there[part], slice(width, width + 128))):
                if add:
                    value = value + held[j, pl.ds(start, pad), lanes].astype(F32)
                held[j, pl.ds(start, pad), lanes] = value.astype(BF)

    @pl.when(g < steps)
    def _():
        for k in range(few):
            last = [k * deep + per - 1, (k + 1) * deep - 1]
            notes = [in_ref[r : r + 1, 0:128].astype(F32) for r in last]
            start = pl.multiple_of((g * few + k) * pad, 16)
            block = in_ref[k * deep : (k + 1) * deep]
            lay(block, places(zn, notes, per, 0, per - 1), start, False)

        @pl.when(flag_ref[0] != 0)
        def _():
            @pl.when(g == 0)
            def _():
                pltpu.sync_copy(more_ref, more_vmem)

            @pl.loop(0, few)
            def _(k):
                pair = g * few + k
                top = pl.multiple_of(k * deep, 16)
                ends = [in_ref[pl.ds(pl.multiple_of(top + (h + 1) * per - 16, 16), 16), 0:128] for h in (0, 1)]
                notes = [e.astype(F32)[15:16] for e in ends]
                start = pl.multiple_of(pair * pad, 16)
                from_row = pl.multiple_of(pair * more_deep, 16)
                lay(more_vmem[pl.ds(from_row, more_deep), :], places(zn, notes, rest, per - 1, rest), start, True)

    @pl.when(g >= steps)
    def _():
        first = (g - steps) * slots
        logits = []
        for k in range(slots):
            panel = panel_ref[k]
            wide = panel.astype(F32)
            sqnorm = jnp.sum(wide * wide, axis=1, keepdims=True)
            logits.append(dot(panel, held[first + k][:, :width], ((1,), (1,))) - 0.5 * sqnorm)
        for k in range(slots):
            peak = jnp.max(logits[k], axis=0, keepdims=True)
            shifted = jnp.exp(logits[k] - peak)
            total = jnp.sum(shifted, axis=0, keepdims=True)
            score_ref[pl.ds(first + k, 1), :] = peak + jnp.log(total)
            weights = (shifted * (1.0 / total)).astype(BF)
            sums = dot(weights, held[first + k])
            sums_ref[k] = sums[:, :width].astype(BF)
            mass_ref[pl.ds(first + k, 1), :] = jnp.transpose(sums[:, width:])[0:1]


def assign(flag, rows, more, panels, pairs, few=8, slots=2):
    zn, fine, width = panels.shape
    deep = rows.shape[0] // pairs
    spread = pairs * 2 * CAP
    steps = pairs // few
    whole = lambda g, f: (0, 0)
    by_slot = lambda g, f: (jnp.maximum(g - steps, 0), 0, 0)
    return pl.pallas_call(
        functools.partial(assign_kernel, steps, zn, few, slots),
        grid_spec=pltpu.PrefetchScalarGridSpec(
            num_scalar_prefetch=1,
            grid=(steps + zn // slots,),
            in_specs=[
                pl.BlockSpec((few * deep, width), lambda g, f: (jnp.minimum(g, steps - 1), 0)),
                pl.BlockSpec(memory_space=pl.ANY),
                pl.BlockSpec((slots, fine, width), by_slot),
            ],
            out_specs=[
                pl.BlockSpec((slots, fine, width), by_slot),
                pl.BlockSpec((zn, fine), whole),
                pl.BlockSpec((zn, spread), whole),
            ],
            scratch_shapes=[
                pltpu.VMEM((zn, spread, width + 128), BF),
                pltpu.VMEM(more.shape, BF),
            ],
        ),
        out_shape=(
            jax.ShapeDtypeStruct((zn, fine, width), BF),
            jax.ShapeDtypeStruct((zn, fine), F32),
            jax.ShapeDtypeStruct((zn, spread), F32),
        ),
        cost_estimate=pl.CostEstimate(
            flops=8 * 10**9, bytes_accessed=2 * 10**7, transcendentals=2 * 10**6
        ),
        name="assign",
    )(flag, rows, more, panels)


def lookup_kernel(place_ref, table_ref, out_ref):
    slots, rows = table_ref.shape[1], place_ref.shape[1]
    table = table_ref[...]
    hi = table.astype(BF)
    rest = table - hi.astype(F32)
    mid = rest.astype(BF)
    low = (rest - mid.astype(F32)).astype(BF)
    hot = onehot(iota((slots, rows), 0) == place_ref[1:2, :])
    value = dot(hi, hot) + dot(mid, hot) + dot(low, hot)
    mine = iota(value.shape, 0) == place_ref[2:3, :]
    out_ref[...] = jnp.sum(jnp.where(mine, value, 0.0), axis=0, keepdims=True)


def lookup(place, table):
    return pl.pallas_call(
        lookup_kernel,
        out_shape=jax.ShapeDtypeStruct((1, place.shape[1]), F32),
        cost_estimate=pl.CostEstimate(flops=10**8, bytes_accessed=10**5, transcendentals=0),
        name="lookup",
    )(place, table)


def exchange(x, axes):
    return lax.all_to_all(x, axes, split_axis=0, concat_axis=0, tiled=True)


def swap_step(x, dim, axis, bit, beside):
    other = 1 - ((lax.axis_index(axis) >> bit) & 1)
    send = lax.dynamic_index_in_dim(x, other, dim, keepdims=True)
    got = lax.ppermute(send, axis, [(i, i ^ (1 << bit)) for i in range(4)])
    got, beside = lax.optimization_barrier((got, beside))
    return lax.dynamic_update_index_in_dim(x, got, other, dim), beside


def local(points, coarse_id, owner_map, centroids):
    zn, cores = lax.axis_size("z"), lax.axis_size("core")
    dpn = lax.axis_size("y") * lax.axis_size("x")
    peers = dpn * cores
    bound = zn * CAP
    rows, width = points.shape

    block = centroids.reshape((2, 2, 2, 2) + centroids.shape[1:])
    found = index(
        coarse_id.reshape(1, rows), owner_map.reshape(1, -1), zn, dpn, cores, bound
    )
    block, (place, note, segment) = swap_step(block, 0, "y", 1, found)
    packed = sort_pack(segment, place, points, note, ROWS, bound, zn, 1024)
    block, packed = swap_step(block, 2, "x", 1, packed)
    arrived = exchange(packed.reshape(peers, ROWS, width), PLANE)
    block, _ = swap_step(block, 1, "y", 0, ())
    block, _ = swap_step(block, 3, "x", 0, ())
    panel = block.reshape(-1, width)
    panels = lax.all_gather(panel, "z", axis=0)

    most = jnp.max(arrived[:, ROWS - 1, zn].astype(F32))

    def second(per):
        block = pack(place, points, peers, per, ROWS - 1, bound, 16 * per)
        block = exchange(block.reshape(peers, per, width), PLANE)
        return jnp.pad(block, ((0, 0), (0, REST - per), (0, 0))).reshape(peers * REST, width)

    level = (most > ROWS - 1).astype(jnp.int32) + (most > ROWS - 1 + SOME).astype(jnp.int32)
    more = lax.switch(
        level,
        (lambda: jnp.zeros((peers * REST, width), BF), lambda: second(SOME), lambda: second(REST)),
    )
    sums, mass, score = assign(
        level.reshape(1), arrived.reshape(peers * ROWS, width), more, panels, peers // 2
    )
    sums = lax.psum_scatter(sums, "z", scatter_dimension=0, tiled=True)[0]
    score = score.reshape(zn, peers, CAP).transpose(1, 0, 2).reshape(peers, zn * CAP)
    score = exchange(score, PLANE).reshape(peers * zn, CAP).T
    point_score = lookup(place, score).reshape(rows)
    mass = jnp.sum(exchange(mass, "z"), axis=0)
    updated = (sums.astype(F32) + PRIOR * panel.astype(F32)) / (mass[:, None] + PRIOR)
    updated = updated.astype(BF).reshape(dpn, -1, width)
    return exchange(updated, ("y", "x")), point_score


def solution(mesh):
    devices = mesh.devices
    chips = Mesh(devices.reshape(4, 4, 8, 2), ("y", "x", "z", "core"))
    every = ("y", "x", "z", "core")
    grid = P(("z", "core"), ("y", "x"), None)
    return jax.shard_map(
        local,
        mesh=chips,
        in_specs=(P(every, None), P(every, None), P(), grid),
        out_specs=(grid, P(every)),
        check_vma=False,
    )
```

```python
import functools
import jax
import jax.numpy as jnp
from jax import lax
from jax.experimental import pallas as pl
from jax.experimental.pallas import tpu as pltpu
from jax.sharding import Mesh, PartitionSpec as P

PRIOR = 4.0
CAP = 24
ROWS = 128
BLOCK = 256
WINDOW = 64
SOME, REST = 16, 72
PLANE = ("y", "x", "core")
BF = jnp.bfloat16
F32 = jnp.float32


def iota(shape, dim):
    return lax.broadcasted_iota(jnp.int32, shape, dim)


def dot(a, b, dims=((1,), (0,))):
    return lax.dot_general(a, b, (dims, ((), ())), preferred_element_type=F32)


def onehot(mask):
    return jnp.where(mask, 1.0, 0.0).astype(BF)


def index_kernel(
    zn, dpn, cores, bound, coarse_ref, owner_ref, place_ref, note_ref, segment_ref, hot_ref
):
    slots = owner_ref.shape[1]
    rows = coarse_ref.shape[1]
    blocks = rows // BLOCK
    peers, width = note_ref.shape
    owner = owner_ref[...]
    column, cluster = owner % dpn, owner // dpn
    lane_of = (column * cores + cluster % cores) * zn + cluster // cores
    move = onehot(iota((slots, slots), 0) == lane_of)
    earlier = onehot(iota((BLOCK, BLOCK), 0) < iota((BLOCK, BLOCK), 1))
    ranks, sizes = [], []
    for b in range(blocks):
        part = slice(b * BLOCK, (b + 1) * BLOCK)
        named = onehot(iota((slots, BLOCK), 0) == coarse_ref[:, part])
        hot = dot(move, named)
        hot_bf = hot.astype(BF)
        hot_ref[:, part] = hot_bf
        ranks.append(jnp.sum(hot * dot(hot_bf, earlier), axis=0, keepdims=True))
        sizes.append(dot(jnp.ones((8, BLOCK), BF), hot_bf, ((1,), (1,)))[0:1])
    rank = jnp.concatenate(ranks, axis=1)
    size = jnp.concatenate(sizes, axis=0)
    done, carry = jnp.zeros((1, slots), F32), []
    for b in range(blocks):
        carry.append(done)
        done = done + sizes[b]
    carry = jnp.concatenate(carry, axis=0)
    la, lb = iota((slots, slots), 0), iota((slots, slots), 1)
    lower = dot(size.astype(BF), onehot(la < lb))
    group = onehot((la // zn == lb // zn) & (la < lb))
    offset = dot(jnp.broadcast_to(done, (8, slots)).astype(BF), group)
    which = iota((8, slots), 0)
    query = jnp.where(which == 0, offset, iota((8, slots), 1).astype(F32))
    query = jnp.concatenate([query, lower, carry], axis=0).astype(BF)
    found = dot(query, hot_ref[...])
    own = iota((blocks, rows), 1) // BLOCK == iota((blocks, rows), 0)
    mine = lambda k: jnp.sum(
        jnp.where(own, found[8 + k * blocks : 8 + (k + 1) * blocks], 0.0), axis=0, keepdims=True
    )
    sort = (rank + mine(0)).astype(jnp.int32)
    rank = (rank + mine(1)).astype(jnp.int32)
    lane = found[1:2].astype(jnp.int32)
    pos = (lane // zn) * bound + found[0:1].astype(jnp.int32) + rank
    row = iota((8, rows), 0)
    place_ref[...] = jnp.where(
        row == 0, pos, jnp.where(row == 1, lane, jnp.where(row == 2, rank, sort))
    )
    segment_ref[:, :slots] = lower.astype(jnp.int32)
    segment_ref[:, slots:] = jnp.full((blocks, 128), BLOCK, jnp.int32)
    mine = iota((peers, slots), 1) // zn == iota((peers, slots), 0)
    spread = jnp.where(mine, done, 0.0)
    most = jnp.max(jnp.sum(spread, axis=1, keepdims=True), axis=0, keepdims=True)
    spot = onehot(iota((slots, width), 0) % zn == iota((slots, width), 1))
    note = dot(spread.astype(BF), spot)
    note_ref[...] = jnp.where(iota((peers, width), 1) == zn, most, note)


def index(coarse, owner, zn, dpn, cores, bound):
    rows, slots = coarse.shape[1], owner.shape[1]
    return pl.pallas_call(
        functools.partial(index_kernel, zn, dpn, cores, bound),
        out_shape=(
            jax.ShapeDtypeStruct((8, rows), jnp.int32),
            jax.ShapeDtypeStruct((dpn * cores, 128), F32),
            jax.ShapeDtypeStruct((rows // BLOCK, slots + 128), jnp.int32),
        ),
        scratch_shapes=[pltpu.VMEM((slots, rows), BF)],
        cost_estimate=pl.CostEstimate(flops=10**9, bytes_accessed=10**5, transcendentals=0),
        name="place",
    )(coarse, owner)


def pack_kernel(per, first, bound, place_ref, points_ref, out_ref):
    g = pl.program_id(0)
    tall = out_ref.shape[0]
    i = iota((tall, 1), 0)
    want = (g * (tall // per) + i // per) * bound + first + i % per
    pick = onehot(place_ref[0:1, :] == want)
    out_ref[...] = dot(pick, points_ref[...]).astype(BF)


def pack(place, points, peers, per, first, bound, tall):
    rows, width = points.shape
    return pl.pallas_call(
        functools.partial(pack_kernel, per, first, bound),
        grid=(peers * per // tall,),
        in_specs=[
            pl.BlockSpec((8, rows), lambda g: (0, 0)),
            pl.BlockSpec((rows, width), lambda g: (0, 0)),
        ],
        out_specs=pl.BlockSpec((tall, width), lambda g: (g, 0)),
        out_shape=jax.ShapeDtypeStruct((peers * per, width), BF),
        cost_estimate=pl.CostEstimate(
            flops=2 * peers * per * rows * width, bytes_accessed=10**7, transcendentals=0
        ),
        name="pack",
    )(place, points)


def sort_pack_kernel(
    per, bound, zn, segment_ref, place_ref, points_ref, note_ref, out_ref, sorted_ref, key_ref,
    near_ref,
):
    g = pl.program_id(0)
    tall = out_ref.shape[0]
    blocks = points_ref.shape[0] // BLOCK
    wide = BLOCK // WINDOW

    @pl.when(g == 0)
    def _():
        for b in range(blocks):
            part = slice(b * BLOCK, (b + 1) * BLOCK)
            move = onehot(iota((BLOCK, BLOCK), 0) == place_ref[3:4, part])
            sorted_ref[part] = dot(move, points_ref[part]).astype(BF)
            key = place_ref[0:1, part]
            which = iota((8, BLOCK), 0)
            halves = jnp.where(which == 0, key // 128, jnp.where(which == 1, key % 128, 0))
            keys = dot(halves.astype(F32).astype(BF), move, ((1,), (1,)))
            key_ref[b : b + 1, :] = (keys[0:1] * 128.0 + keys[1:2]).astype(jnp.int32)

    both = 2 * per
    i = iota((both, 1), 0)
    lane = iota((1, BLOCK), 1)

    def picked(q, group, starts, news):
        want = (group * 2 + i // per) * bound + i % per
        keys = []
        for b in range(blocks):
            rows = pl.multiple_of(b * BLOCK + starts[b], 16)
            near_ref[q, b * WINDOW : (b + 1) * WINDOW, :] = sorted_ref[pl.ds(rows, WINDOW), :]
            key = key_ref[b : b + 1, :]
            if news is not None:
                key = jnp.where(lane >= news[b], key, -1)
            shift = (b % wide) * WINDOW + BLOCK - starts[b]
            key = pltpu.roll(key, shift % BLOCK, 1)
            if b % wide == 0:
                keys.append(key)
            else:
                keys[-1] = jnp.where(lane >= (b % wide) * WINDOW, key, keys[-1])
        pick = onehot(jnp.concatenate(keys, axis=1) == want)
        return dot(pick, near_ref[q])

    groups = tall // both
    longest, lows_of = jnp.int32(0), []
    for q in range(groups):
        first = (g * groups + q) * 2 * zn
        lows = [segment_ref[b, first] // 16 * 16 for b in range(blocks)]
        highs = [segment_ref[b, first + 2 * zn] for b in range(blocks)]
        for low, high in zip(lows, highs):
            longest = jnp.maximum(longest, high - low)
        lows_of.append(lows)
        starts = [jnp.minimum(low, BLOCK - WINDOW) for low in lows]
        out_ref[q * both : (q + 1) * both] = picked(q, g * groups + q, starts, None).astype(BF)

    @pl.when(longest > WINDOW)
    def _():
        @pl.loop(1, (longest + WINDOW - 1) // WINDOW)
        def _(w):
            for q in range(groups):
                here = slice(q * both, (q + 1) * both)
                news = [low + w * WINDOW for low in lows_of[q]]
                starts = [jnp.minimum(new, BLOCK - WINDOW) for new in news]
                more = picked(q, g * groups + q, starts, news)
                out_ref[here] = (out_ref[here].astype(F32) + more).astype(BF)

    for k in range(tall // per):
        tile = slice((k + 1) * per - 16, (k + 1) * per)
        note = jnp.broadcast_to(note_ref[k : k + 1], (16, 128))
        end = iota((16, 128), 0) == 15
        out_ref[tile, :128] = jnp.where(end, note, out_ref[tile, :128].astype(F32)).astype(BF)


def sort_pack(segment, place, points, note, per, bound, zn, tall):
    rows, width = points.shape
    peers = note.shape[0]
    blocks = rows // BLOCK
    return pl.pallas_call(
        functools.partial(sort_pack_kernel, per, bound, zn),
        grid_spec=pltpu.PrefetchScalarGridSpec(
            num_scalar_prefetch=1,
            grid=(peers * per // tall,),
            in_specs=[
                pl.BlockSpec((8, rows), lambda g, s: (0, 0)),
                pl.BlockSpec((rows, width), lambda g, s: (0, 0)),
                pl.BlockSpec((tall // per, 128), lambda g, s: (g, 0)),
            ],
            out_specs=pl.BlockSpec((tall, width), lambda g, s: (g, 0)),
            scratch_shapes=[
                pltpu.VMEM((rows, width), BF),
                pltpu.VMEM((blocks, BLOCK), jnp.int32),
                pltpu.VMEM((tall // (2 * per), blocks * WINDOW, width), BF),
            ],
        ),
        out_shape=jax.ShapeDtypeStruct((peers * per, width), BF),
        cost_estimate=pl.CostEstimate(
            flops=5 * 10**9, bytes_accessed=10**7, transcendentals=0
        ),
        name="sort_pack",
    )(segment, place, points, note)


def places(zn, notes, per, first, count):
    lane, sub = iota((zn, 128), 1), iota((zn, 128), 0)
    sides = []
    for note in notes:
        note = jnp.broadcast_to(note, (zn, 128))
        ends = jnp.sum(jnp.where(lane <= sub, note, 0.0), axis=1, keepdims=True)
        size = jnp.sum(jnp.where(lane == sub, note, 0.0), axis=1, keepdims=True)
        sides.append((ends, size))
    c = iota((zn, 2 * per), 1)
    second = c >= per
    at = c - jnp.where(second, per, 0)
    pos = (at + first).astype(F32)
    passed = pos >= jnp.where(second, sides[1][0], sides[0][0])
    size = jnp.where(second, sides[1][1], sides[0][1])
    slot = jnp.sum(jnp.where(passed, 1.0, 0.0), axis=0, keepdims=True)
    begin = jnp.sum(jnp.where(passed, size, 0.0), axis=0, keepdims=True)
    side = jnp.where(second[0:1], 1.0 * CAP, 0.0)
    dest = slot * (2 * CAP) + side + pos[0:1] - begin
    return jnp.where(at[0:1] < count, dest, -1.0).astype(jnp.int32), [size for _, size in sides]


def assign_kernel(
    steps, zn, few, slots, flag_ref, in_ref, more_ref, panel_ref, sums_ref, mass_ref, score_ref,
    held, counts, live, more_vmem,
):
    g = pl.program_id(0)
    pad = 2 * CAP
    tall = zn * pad
    width = in_ref.shape[1]
    deep, more_deep = in_ref.shape[0] // few, more_vmem.shape[0] // (steps * few)
    per, rest = deep // 2, more_deep // 2

    def lay(block, dest, start, add):
        laid = dot(onehot(iota((tall, block.shape[0]), 0) == dest), block)
        for j in range(zn):
            value = laid[j * pad : (j + 1) * pad]
            if add:
                value = value + held[j, pl.ds(start, pad), :].astype(F32)
            held[j, pl.ds(start, pad), :] = value.astype(BF)

    @pl.when(g == 0)
    def _():
        counts[...] = jnp.zeros_like(counts)

    @pl.when(g < steps)
    def _():
        senders = counts[...]
        for k in range(few):
            last = [k * deep + per - 1, (k + 1) * deep - 1]
            notes = [in_ref[r : r + 1, 0:128].astype(F32) for r in last]
            start = pl.multiple_of((g * few + k) * pad, 16)
            block = in_ref[k * deep : (k + 1) * deep]
            dest, sizes = places(zn, notes, per, 0, per - 1)
            for h in (0, 1):
                sender = (g * few + k) * 2 + h
                senders = jnp.where(iota(senders.shape, 1) == sender, sizes[h], senders)
            lay(block, dest, start, False)
        counts[...] = senders

        @pl.when(flag_ref[0] != 0)
        def _():
            @pl.when(g == 0)
            def _():
                pltpu.sync_copy(more_ref, more_vmem)

            @pl.loop(0, few)
            def _(k):
                pair = g * few + k
                top = pl.multiple_of(k * deep, 16)
                ends = [in_ref[pl.ds(pl.multiple_of(top + (h + 1) * per - 16, 16), 16), 0:128] for h in (0, 1)]
                notes = [e.astype(F32)[15:16] for e in ends]
                start = pl.multiple_of(pair * pad, 16)
                from_row = pl.multiple_of(pair * more_deep, 16)
                dest, _ = places(zn, notes, rest, per - 1, rest)
                lay(more_vmem[pl.ds(from_row, more_deep), :], dest, start, True)

    @pl.when(g == steps)
    def _():
        spread = (counts.shape[1], live.shape[1])
        of_sender = dot(
            counts[...].astype(BF), onehot(iota(spread, 1) // CAP == iota(spread, 0))
        )
        live[...] = jnp.where((iota(live.shape, 1) % CAP).astype(F32) < of_sender, 1.0, 0.0)

    @pl.when(g >= steps)
    def _():
        first = (g - steps) * slots
        logits = []
        for k in range(slots):
            panel = panel_ref[k]
            wide = panel.astype(F32)
            sqnorm = jnp.sum(wide * wide, axis=1, keepdims=True)
            logits.append(dot(panel, held[first + k], ((1,), (1,))) - 0.5 * sqnorm)
        for k in range(slots):
            peak = jnp.max(logits[k], axis=0, keepdims=True)
            shifted = jnp.exp(logits[k] - peak)
            total = jnp.sum(shifted, axis=0, keepdims=True)
            score_ref[pl.ds(first + k, 1), :] = peak + jnp.log(total)
            there = live[pl.ds(first + k, 1), :] > 0
            weights = jnp.where(there, shifted * (1.0 / total), 0.0).astype(BF)
            mass = jnp.sum(weights.astype(F32), axis=1, keepdims=True)
            mass = jnp.transpose(jnp.broadcast_to(mass, (mass.shape[0], 128)))
            mass_ref[pl.ds(first + k, 1), :] = mass[0:1]
            sums_ref[k] = dot(weights, held[first + k]).astype(BF)


def assign(flag, rows, more, panels, pairs, few=8, slots=2):
    zn, fine, width = panels.shape
    deep = rows.shape[0] // pairs
    spread = pairs * 2 * CAP
    steps = pairs // few
    whole = lambda g, f: (0, 0)
    by_slot = lambda g, f: (jnp.maximum(g - steps, 0), 0, 0)
    return pl.pallas_call(
        functools.partial(assign_kernel, steps, zn, few, slots),
        grid_spec=pltpu.PrefetchScalarGridSpec(
            num_scalar_prefetch=1,
            grid=(steps + zn // slots,),
            in_specs=[
                pl.BlockSpec((few * deep, width), lambda g, f: (jnp.minimum(g, steps - 1), 0)),
                pl.BlockSpec(memory_space=pl.ANY),
                pl.BlockSpec((slots, fine, width), by_slot),
            ],
            out_specs=[
                pl.BlockSpec((slots, fine, width), by_slot),
                pl.BlockSpec((zn, fine), whole),
                pl.BlockSpec((zn, spread), whole),
            ],
            scratch_shapes=[
                pltpu.VMEM((zn, spread, width), BF),
                pltpu.VMEM((zn, 128), F32),
                pltpu.VMEM((zn, spread), F32),
                pltpu.VMEM(more.shape, BF),
            ],
        ),
        out_shape=(
            jax.ShapeDtypeStruct((zn, fine, width), BF),
            jax.ShapeDtypeStruct((zn, fine), F32),
            jax.ShapeDtypeStruct((zn, spread), F32),
        ),
        cost_estimate=pl.CostEstimate(
            flops=8 * 10**9, bytes_accessed=2 * 10**7, transcendentals=2 * 10**6
        ),
        name="assign",
    )(flag, rows, more, panels)


def lookup_kernel(place_ref, table_ref, out_ref):
    slots, rows = table_ref.shape[1], place_ref.shape[1]
    table = table_ref[...]
    hi = table.astype(BF)
    rest = table - hi.astype(F32)
    mid = rest.astype(BF)
    low = (rest - mid.astype(F32)).astype(BF)
    hot = onehot(iota((slots, rows), 0) == place_ref[1:2, :])
    value = dot(hi, hot) + dot(mid, hot) + dot(low, hot)
    mine = iota(value.shape, 0) == place_ref[2:3, :]
    out_ref[...] = jnp.sum(jnp.where(mine, value, 0.0), axis=0, keepdims=True)


def lookup(place, table):
    return pl.pallas_call(
        lookup_kernel,
        out_shape=jax.ShapeDtypeStruct((1, place.shape[1]), F32),
        cost_estimate=pl.CostEstimate(flops=10**8, bytes_accessed=10**5, transcendentals=0),
        name="lookup",
    )(place, table)


def exchange(x, axes):
    return lax.all_to_all(x, axes, split_axis=0, concat_axis=0, tiled=True)


def local(points, coarse_id, owner_map, centroids):
    zn, cores = lax.axis_size("z"), lax.axis_size("core")
    dpn = lax.axis_size("y") * lax.axis_size("x")
    peers = dpn * cores
    bound = zn * CAP
    rows, width = points.shape

    panel = exchange(centroids, ("y", "x")).reshape(-1, width)
    place, note, segment = index(
        coarse_id.reshape(1, rows), owner_map.reshape(1, -1), zn, dpn, cores, bound
    )
    packed = sort_pack(segment, place, points, note, ROWS, bound, zn, 1024)
    arrived = exchange(packed.reshape(peers, ROWS, width), PLANE)
    panels = lax.all_gather(panel, "z", axis=0)

    most = jnp.max(arrived[:, ROWS - 1, zn].astype(F32))

    def second(per):
        block = pack(place, points, peers, per, ROWS - 1, bound, 16 * per)
        block = exchange(block.reshape(peers, per, width), PLANE)
        return jnp.pad(block, ((0, 0), (0, REST - per), (0, 0))).reshape(peers * REST, width)

    level = (most > ROWS - 1).astype(jnp.int32) + (most > ROWS - 1 + SOME).astype(jnp.int32)
    more = lax.switch(
        level,
        (lambda: jnp.zeros((peers * REST, width), BF), lambda: second(SOME), lambda: second(REST)),
    )
    sums, mass, score = assign(
        level.reshape(1), arrived.reshape(peers * ROWS, width), more, panels, peers // 2
    )
    sums = lax.psum_scatter(sums, "z", scatter_dimension=0, tiled=True)[0]
    score = score.reshape(zn, peers, CAP).transpose(1, 0, 2).reshape(peers, zn * CAP)
    score = exchange(score, PLANE).reshape(peers * zn, CAP).T
    point_score = lookup(place, score).reshape(rows)
    mass = mass.reshape(zn, dpn, -1).transpose(1, 0, 2).reshape(dpn * zn, -1)
    mass = jnp.sum(exchange(mass, ("y", "x", "z")).reshape(dpn, zn, -1), axis=1)
    sums = exchange(sums.reshape(dpn, -1, width), ("y", "x"))
    updated = (sums.astype(F32) + PRIOR * centroids.astype(F32)) / (mass[..., None] + PRIOR)
    return updated.astype(BF), point_score


def solution(mesh):
    devices = mesh.devices
    chips = Mesh(devices.reshape(4, 4, 8, 2), ("y", "x", "z", "core"))
    every = ("y", "x", "z", "core")
    grid = P(("z", "core"), ("y", "x"), None)
    return jax.shard_map(
        local,
        mesh=chips,
        in_specs=(P(every, None), P(every, None), P(), grid),
        out_specs=(grid, P(every)),
        check_vma=False,
    )
```

```python
import functools
import jax
import jax.numpy as jnp
from jax import lax
from jax.experimental import pallas as pl
from jax.experimental.pallas import tpu as pltpu
from jax.sharding import Mesh, PartitionSpec as P

PRIOR = 4.0
CAP = 24
ROWS = 128
BLOCK = 256
WINDOW = 64
SOME, REST = 16, 72
PLANE = ("y", "x", "core")
BF = jnp.bfloat16
F32 = jnp.float32


def iota(shape, dim):
    return lax.broadcasted_iota(jnp.int32, shape, dim)


def dot(a, b, dims=((1,), (0,))):
    return lax.dot_general(a, b, (dims, ((), ())), preferred_element_type=F32)


def onehot(mask):
    return jnp.where(mask, 1.0, 0.0).astype(BF)


def index_kernel(
    zn, dpn, cores, bound, coarse_ref, owner_ref, place_ref, note_ref, segment_ref, hot_ref
):
    slots = owner_ref.shape[1]
    rows = coarse_ref.shape[1]
    blocks = rows // BLOCK
    peers, width = note_ref.shape
    owner = owner_ref[...]
    column, cluster = owner % dpn, owner // dpn
    lane_of = (column * cores + cluster % cores) * zn + cluster // cores
    move = onehot(iota((slots, slots), 0) == lane_of)
    earlier = onehot(iota((BLOCK, BLOCK), 0) < iota((BLOCK, BLOCK), 1))
    ranks, sizes = [], []
    for b in range(blocks):
        part = slice(b * BLOCK, (b + 1) * BLOCK)
        named = onehot(iota((slots, BLOCK), 0) == coarse_ref[:, part])
        hot = dot(move, named)
        hot_bf = hot.astype(BF)
        hot_ref[:, part] = hot_bf
        ranks.append(jnp.sum(hot * dot(hot_bf, earlier), axis=0, keepdims=True))
        sizes.append(dot(jnp.ones((8, BLOCK), BF), hot_bf, ((1,), (1,)))[0:1])
    rank = jnp.concatenate(ranks, axis=1)
    size = jnp.concatenate(sizes, axis=0)
    done, carry = jnp.zeros((1, slots), F32), []
    for b in range(blocks):
        carry.append(done)
        done = done + sizes[b]
    carry = jnp.concatenate(carry, axis=0)
    la, lb = iota((slots, slots), 0), iota((slots, slots), 1)
    lower = dot(size.astype(BF), onehot(la < lb))
    group = onehot((la // zn == lb // zn) & (la < lb))
    offset = dot(jnp.broadcast_to(done, (8, slots)).astype(BF), group)
    which = iota((8, slots), 0)
    query = jnp.where(which == 0, offset, iota((8, slots), 1).astype(F32))
    query = jnp.concatenate([query, lower, carry], axis=0).astype(BF)
    found = dot(query, hot_ref[...])
    own = iota((blocks, rows), 1) // BLOCK == iota((blocks, rows), 0)
    mine = lambda k: jnp.sum(
        jnp.where(own, found[8 + k * blocks : 8 + (k + 1) * blocks], 0.0), axis=0, keepdims=True
    )
    sort = (rank + mine(0)).astype(jnp.int32)
    rank = (rank + mine(1)).astype(jnp.int32)
    lane = found[1:2].astype(jnp.int32)
    pos = (lane // zn) * bound + found[0:1].astype(jnp.int32) + rank
    row = iota((8, rows), 0)
    place_ref[...] = jnp.where(
        row == 0, pos, jnp.where(row == 1, lane, jnp.where(row == 2, rank, sort))
    )
    segment_ref[:, :slots] = lower.astype(jnp.int32)
    segment_ref[:, slots:] = jnp.full((blocks, 128), BLOCK, jnp.int32)
    mine = iota((peers, slots), 1) // zn == iota((peers, slots), 0)
    spread = jnp.where(mine, done, 0.0)
    most = jnp.max(jnp.sum(spread, axis=1, keepdims=True), axis=0, keepdims=True)
    spot = onehot(iota((slots, width), 0) % zn == iota((slots, width), 1))
    note = dot(spread.astype(BF), spot)
    note_ref[...] = jnp.where(iota((peers, width), 1) == zn, most, note)


def index(coarse, owner, zn, dpn, cores, bound):
    rows, slots = coarse.shape[1], owner.shape[1]
    return pl.pallas_call(
        functools.partial(index_kernel, zn, dpn, cores, bound),
        out_shape=(
            jax.ShapeDtypeStruct((8, rows), jnp.int32),
            jax.ShapeDtypeStruct((dpn * cores, 128), F32),
            jax.ShapeDtypeStruct((rows // BLOCK, slots + 128), jnp.int32),
        ),
        scratch_shapes=[pltpu.VMEM((slots, rows), BF)],
        cost_estimate=pl.CostEstimate(flops=10**9, bytes_accessed=10**5, transcendentals=0),
        name="place",
    )(coarse, owner)


def pack_kernel(per, first, bound, place_ref, points_ref, out_ref):
    g = pl.program_id(0)
    tall = out_ref.shape[0]
    i = iota((tall, 1), 0)
    want = (g * (tall // per) + i // per) * bound + first + i % per
    pick = onehot(place_ref[0:1, :] == want)
    out_ref[...] = dot(pick, points_ref[...]).astype(BF)


def pack(place, points, peers, per, first, bound, tall):
    rows, width = points.shape
    return pl.pallas_call(
        functools.partial(pack_kernel, per, first, bound),
        grid=(peers * per // tall,),
        in_specs=[
            pl.BlockSpec((8, rows), lambda g: (0, 0)),
            pl.BlockSpec((rows, width), lambda g: (0, 0)),
        ],
        out_specs=pl.BlockSpec((tall, width), lambda g: (g, 0)),
        out_shape=jax.ShapeDtypeStruct((peers * per, width), BF),
        cost_estimate=pl.CostEstimate(
            flops=2 * peers * per * rows * width, bytes_accessed=10**7, transcendentals=0
        ),
        name="pack",
    )(place, points)


def sort_pack_kernel(
    per, bound, zn, segment_ref, place_ref, points_ref, note_ref, out_ref, sorted_ref, key_ref,
    near_ref,
):
    g = pl.program_id(0)
    tall = out_ref.shape[0]
    blocks = points_ref.shape[0] // BLOCK
    wide = BLOCK // WINDOW

    @pl.when(g == 0)
    def _():
        for b in range(blocks):
            part = slice(b * BLOCK, (b + 1) * BLOCK)
            move = onehot(iota((BLOCK, BLOCK), 0) == place_ref[3:4, part])
            sorted_ref[part] = dot(move, points_ref[part]).astype(BF)
            key = place_ref[0:1, part]
            which = iota((8, BLOCK), 0)
            halves = jnp.where(which == 0, key // 128, jnp.where(which == 1, key % 128, 0))
            keys = dot(halves.astype(F32).astype(BF), move, ((1,), (1,)))
            key_ref[b : b + 1, :] = (keys[0:1] * 128.0 + keys[1:2]).astype(jnp.int32)

    both = 2 * per
    i = iota((both, 1), 0)
    lane = iota((1, BLOCK), 1)

    def picked(q, group, starts, news):
        want = (group * 2 + i // per) * bound + i % per
        keys = []
        for b in range(blocks):
            rows = pl.multiple_of(b * BLOCK + starts[b], 16)
            near_ref[q, b * WINDOW : (b + 1) * WINDOW, :] = sorted_ref[pl.ds(rows, WINDOW), :]
            key = key_ref[b : b + 1, :]
            if news is not None:
                key = jnp.where(lane >= news[b], key, -1)
            shift = (b % wide) * WINDOW + BLOCK - starts[b]
            key = pltpu.roll(key, shift % BLOCK, 1)
            if b % wide == 0:
                keys.append(key)
            else:
                keys[-1] = jnp.where(lane >= (b % wide) * WINDOW, key, keys[-1])
        pick = onehot(jnp.concatenate(keys, axis=1) == want)
        return dot(pick, near_ref[q])

    groups = tall // both
    longest, lows_of = jnp.int32(0), []
    for q in range(groups):
        first = (g * groups + q) * 2 * zn
        lows = [segment_ref[b, first] // 16 * 16 for b in range(blocks)]
        highs = [segment_ref[b, first + 2 * zn] for b in range(blocks)]
        for low, high in zip(lows, highs):
            longest = jnp.maximum(longest, high - low)
        lows_of.append(lows)
        starts = [jnp.minimum(low, BLOCK - WINDOW) for low in lows]
        out_ref[q * both : (q + 1) * both] = picked(q, g * groups + q, starts, None).astype(BF)

    @pl.when(longest > WINDOW)
    def _():
        @pl.loop(1, (longest + WINDOW - 1) // WINDOW)
        def _(w):
            for q in range(groups):
                here = slice(q * both, (q + 1) * both)
                news = [low + w * WINDOW for low in lows_of[q]]
                starts = [jnp.minimum(new, BLOCK - WINDOW) for new in news]
                more = picked(q, g * groups + q, starts, news)
                out_ref[here] = (out_ref[here].astype(F32) + more).astype(BF)

    for k in range(tall // per):
        tile = slice((k + 1) * per - 16, (k + 1) * per)
        note = jnp.broadcast_to(note_ref[k : k + 1], (16, 128))
        end = iota((16, 128), 0) == 15
        out_ref[tile, :128] = jnp.where(end, note, out_ref[tile, :128].astype(F32)).astype(BF)


def sort_pack(segment, place, points, note, per, bound, zn, tall):
    rows, width = points.shape
    peers = note.shape[0]
    blocks = rows // BLOCK
    return pl.pallas_call(
        functools.partial(sort_pack_kernel, per, bound, zn),
        grid_spec=pltpu.PrefetchScalarGridSpec(
            num_scalar_prefetch=1,
            grid=(peers * per // tall,),
            in_specs=[
                pl.BlockSpec((8, rows), lambda g, s: (0, 0)),
                pl.BlockSpec((rows, width), lambda g, s: (0, 0)),
                pl.BlockSpec((tall // per, 128), lambda g, s: (g, 0)),
            ],
            out_specs=pl.BlockSpec((tall, width), lambda g, s: (g, 0)),
            scratch_shapes=[
                pltpu.VMEM((rows, width), BF),
                pltpu.VMEM((blocks, BLOCK), jnp.int32),
                pltpu.VMEM((tall // (2 * per), blocks * WINDOW, width), BF),
            ],
        ),
        out_shape=jax.ShapeDtypeStruct((peers * per, width), BF),
        cost_estimate=pl.CostEstimate(
            flops=5 * 10**9, bytes_accessed=10**7, transcendentals=0
        ),
        name="sort_pack",
    )(segment, place, points, note)


def places(zn, notes, per, first, count):
    lane, sub = iota((zn, 128), 1), iota((zn, 128), 0)
    sides = []
    for note in notes:
        note = jnp.broadcast_to(note, (zn, 128))
        ends = jnp.sum(jnp.where(lane <= sub, note, 0.0), axis=1, keepdims=True)
        size = jnp.sum(jnp.where(lane == sub, note, 0.0), axis=1, keepdims=True)
        sides.append((ends, size))
    c = iota((zn, 2 * per), 1)
    second = c >= per
    at = c - jnp.where(second, per, 0)
    pos = (at + first).astype(F32)
    passed = pos >= jnp.where(second, sides[1][0], sides[0][0])
    size = jnp.where(second, sides[1][1], sides[0][1])
    slot = jnp.sum(jnp.where(passed, 1.0, 0.0), axis=0, keepdims=True)
    begin = jnp.sum(jnp.where(passed, size, 0.0), axis=0, keepdims=True)
    side = jnp.where(second[0:1], 1.0 * CAP, 0.0)
    dest = slot * (2 * CAP) + side + pos[0:1] - begin
    return jnp.where(at[0:1] < count, dest, -1.0).astype(jnp.int32), [size for _, size in sides]


def assign_kernel(
    steps, zn, few, slots, flag_ref, in_ref, more_ref, panel_ref, sums_ref, mass_ref, score_ref,
    held, counts, live, more_vmem,
):
    g = pl.program_id(0)
    pad = 2 * CAP
    tall = zn * pad
    width = in_ref.shape[1]
    deep, more_deep = in_ref.shape[0] // few, more_vmem.shape[0] // (steps * few)
    per, rest = deep // 2, more_deep // 2

    def lay(block, dest, start, add):
        laid = dot(onehot(iota((tall, block.shape[0]), 0) == dest), block)
        for j in range(zn):
            value = laid[j * pad : (j + 1) * pad]
            if add:
                value = value + held[j, pl.ds(start, pad), :].astype(F32)
            held[j, pl.ds(start, pad), :] = value.astype(BF)

    @pl.when(g == 0)
    def _():
        counts[...] = jnp.zeros_like(counts)

    @pl.when(g < steps)
    def _():
        senders = counts[...]
        for k in range(few):
            last = [k * deep + per - 1, (k + 1) * deep - 1]
            notes = [in_ref[r : r + 1, 0:128].astype(F32) for r in last]
            start = pl.multiple_of((g * few + k) * pad, 16)
            block = in_ref[k * deep : (k + 1) * deep]
            dest, sizes = places(zn, notes, per, 0, per - 1)
            for h in (0, 1):
                sender = (g * few + k) * 2 + h
                senders = jnp.where(iota(senders.shape, 1) == sender, sizes[h], senders)
            lay(block, dest, start, False)
        counts[...] = senders

        @pl.when(flag_ref[0] != 0)
        def _():
            @pl.when(g == 0)
            def _():
                pltpu.sync_copy(more_ref, more_vmem)

            @pl.loop(0, few)
            def _(k):
                pair = g * few + k
                top = pl.multiple_of(k * deep, 16)
                ends = [in_ref[pl.ds(pl.multiple_of(top + (h + 1) * per - 16, 16), 16), 0:128] for h in (0, 1)]
                notes = [e.astype(F32)[15:16] for e in ends]
                start = pl.multiple_of(pair * pad, 16)
                from_row = pl.multiple_of(pair * more_deep, 16)
                dest, sizes = places(zn, notes, rest, per - 1, rest)

                @pl.when(jnp.maximum(jnp.sum(sizes[0]), jnp.sum(sizes[1])) > per - 1)
                def _():
                    lay(more_vmem[pl.ds(from_row, more_deep), :], dest, start, True)

    @pl.when(g == steps)
    def _():
        spread = (counts.shape[1], live.shape[1])
        of_sender = dot(
            counts[...].astype(BF), onehot(iota(spread, 1) // CAP == iota(spread, 0))
        )
        live[...] = jnp.where((iota(live.shape, 1) % CAP).astype(F32) < of_sender, 1.0, 0.0)

    @pl.when(g >= steps)
    def _():
        first = (g - steps) * slots
        logits = []
        for k in range(slots):
            panel = panel_ref[k]
            wide = panel.astype(F32)
            sqnorm = jnp.sum(wide * wide, axis=1, keepdims=True)
            logits.append(dot(panel, held[first + k], ((1,), (1,))) - 0.5 * sqnorm)
        for k in range(slots):
            peak = jnp.max(logits[k], axis=0, keepdims=True)
            shifted = jnp.exp(logits[k] - peak)
            total = jnp.sum(shifted, axis=0, keepdims=True)
            score_ref[pl.ds(first + k, 1), :] = peak + jnp.log(total)
            there = live[pl.ds(first + k, 1), :] > 0
            weights = jnp.where(there, shifted * (1.0 / total), 0.0).astype(BF)
            mass = jnp.sum(weights.astype(F32), axis=1, keepdims=True)
            mass = jnp.transpose(jnp.broadcast_to(mass, (mass.shape[0], 128)))
            mass_ref[pl.ds(first + k, 1), :] = mass[0:1]
            sums_ref[k] = dot(weights, held[first + k]).astype(BF)


def assign(flag, rows, more, panels, pairs, few=8, slots=2):
    zn, fine, width = panels.shape
    deep = rows.shape[0] // pairs
    spread = pairs * 2 * CAP
    steps = pairs // few
    whole = lambda g, f: (0, 0)
    by_slot = lambda g, f: (jnp.maximum(g - steps, 0), 0, 0)
    return pl.pallas_call(
        functools.partial(assign_kernel, steps, zn, few, slots),
        grid_spec=pltpu.PrefetchScalarGridSpec(
            num_scalar_prefetch=1,
            grid=(steps + zn // slots,),
            in_specs=[
                pl.BlockSpec((few * deep, width), lambda g, f: (jnp.minimum(g, steps - 1), 0)),
                pl.BlockSpec(memory_space=pl.ANY),
                pl.BlockSpec((slots, fine, width), by_slot),
            ],
            out_specs=[
                pl.BlockSpec((slots, fine, width), by_slot),
                pl.BlockSpec((zn, fine), whole),
                pl.BlockSpec((zn, spread), whole),
            ],
            scratch_shapes=[
                pltpu.VMEM((zn, spread, width), BF),
                pltpu.VMEM((zn, 128), F32),
                pltpu.VMEM((zn, spread), F32),
                pltpu.VMEM(more.shape, BF),
            ],
        ),
        out_shape=(
            jax.ShapeDtypeStruct((zn, fine, width), BF),
            jax.ShapeDtypeStruct((zn, fine), F32),
            jax.ShapeDtypeStruct((zn, spread), F32),
        ),
        cost_estimate=pl.CostEstimate(
            flops=8 * 10**9, bytes_accessed=2 * 10**7, transcendentals=2 * 10**6
        ),
        name="assign",
    )(flag, rows, more, panels)


def lookup_kernel(place_ref, table_ref, out_ref):
    slots, rows = table_ref.shape[1], place_ref.shape[1]
    table = table_ref[...]
    hi = table.astype(BF)
    rest = table - hi.astype(F32)
    mid = rest.astype(BF)
    low = (rest - mid.astype(F32)).astype(BF)
    hot = onehot(iota((slots, rows), 0) == place_ref[1:2, :])
    value = dot(hi, hot) + dot(mid, hot) + dot(low, hot)
    mine = iota(value.shape, 0) == place_ref[2:3, :]
    out_ref[...] = jnp.sum(jnp.where(mine, value, 0.0), axis=0, keepdims=True)


def lookup(place, table):
    return pl.pallas_call(
        lookup_kernel,
        out_shape=jax.ShapeDtypeStruct((1, place.shape[1]), F32),
        cost_estimate=pl.CostEstimate(flops=10**8, bytes_accessed=10**5, transcendentals=0),
        name="lookup",
    )(place, table)


def exchange(x, axes):
    return lax.all_to_all(x, axes, split_axis=0, concat_axis=0, tiled=True)


def local(points, coarse_id, owner_map, centroids):
    zn, cores = lax.axis_size("z"), lax.axis_size("core")
    dpn = lax.axis_size("y") * lax.axis_size("x")
    peers = dpn * cores
    bound = zn * CAP
    rows, width = points.shape

    panel = exchange(centroids, ("y", "x")).reshape(-1, width)
    place, note, segment = index(
        coarse_id.reshape(1, rows), owner_map.reshape(1, -1), zn, dpn, cores, bound
    )
    packed = sort_pack(segment, place, points, note, ROWS, bound, zn, 1024)
    arrived = exchange(packed.reshape(peers, ROWS, width), PLANE)
    panels = lax.all_gather(panel, "z", axis=0)

    most = jnp.max(arrived[:, ROWS - 1, zn].astype(F32))

    def second(per):
        block = pack(place, points, peers, per, ROWS - 1, bound, 16 * per)
        block = exchange(block.reshape(peers, per, width), PLANE)
        return jnp.pad(block, ((0, 0), (0, REST - per), (0, 0))).reshape(peers * REST, width)

    level = (most > ROWS - 1).astype(jnp.int32) + (most > ROWS - 1 + SOME).astype(jnp.int32)
    more = lax.switch(
        level,
        (lambda: jnp.zeros((peers * REST, width), BF), lambda: second(SOME), lambda: second(REST)),
    )
    sums, mass, score = assign(
        level.reshape(1), arrived.reshape(peers * ROWS, width), more, panels, peers // 2
    )
    sums = lax.psum_scatter(sums, "z", scatter_dimension=0, tiled=True)[0]
    score = score.reshape(zn, peers, CAP).transpose(1, 0, 2).reshape(peers, zn * CAP)
    score = exchange(score, PLANE).reshape(peers * zn, CAP).T
    point_score = lookup(place, score).reshape(rows)
    mass = mass.reshape(zn, dpn, -1).transpose(1, 0, 2).reshape(dpn * zn, -1)
    mass = jnp.sum(exchange(mass, ("y", "x", "z")).reshape(dpn, zn, -1), axis=1)
    sums = exchange(sums.reshape(dpn, -1, width), ("y", "x"))
    updated = (sums.astype(F32) + PRIOR * centroids.astype(F32)) / (mass[..., None] + PRIOR)
    return updated.astype(BF), point_score


def solution(mesh):
    devices = mesh.devices
    chips = Mesh(devices.reshape(4, 4, 8, 2), ("y", "x", "z", "core"))
    every = ("y", "x", "z", "core")
    grid = P(("z", "core"), ("y", "x"), None)
    return jax.shard_map(
        local,
        mesh=chips,
        in_specs=(P(every, None), P(every, None), P(), grid),
        out_specs=(grid, P(every)),
        check_vma=False,
    )
```
